128 devices in a mesh: ctx: 16 (over z_hi, y, core), fsdp: 8 (over z_lo, x).
Axes of the slice: x: 4, y: 4, z: 4 (z_hi: 2, z_lo: 2; z = z_hi * 2 + z_lo), core: 2. Of those that a mesh axis runs over, the one named last changes fastest.
Arguments:
- tokens: bfloat16 [8, 4096, 3072], P('fsdp', 'ctx'), may hold values from -6 to 6
- norm_gain: float32 [3072], replicated, may hold values from 0.1 to 1.9
- qkv_weight: bfloat16 [3072, 2560], P('fsdp'), may hold values from -4 to 4
- block_mask: int32 [32, 32], replicated, may hold values from 0 to 1, as said below
- out_grad: bfloat16 [8, 4096, 1536], P('fsdp', 'ctx'), may hold values from -6 to 6
Outputs:
- attended: bfloat16 [8, 4096, 1536], P('fsdp', 'ctx')
- token_grad: bfloat16 [8, 4096, 3072], P('fsdp', 'ctx')
The draws below stay inside these ranges and needn't reach their ends.
Inputs may be any that keep to these rules, and one draw needn't show every extreme that they name: `block_mask`: every block row has ones on its diagonal and beside it where those blocks exist; exactly one block row is all ones and its block column is all ones too; every other block row has at most 6 ones.
All inputs are finite; a program needn't handle non-finite values.
Results may differ from the reference program's by a relative error of at most 0.019.
Values may be sent and summed in bfloat16 or wider, within the bound.
A program may use at most 128 MiB of HBM per device.

```python
import math
import jax
import jax.numpy as jnp
from jax import lax

D = 3072
HEADS = 12
KV_HEADS = 4
HEAD_DIM = 128
BLOCK = 128
SEQ = 4096
BATCH = 8
NBLK = 32
QW = 1536
KW = 512


def draw_qkv_weight(key, part):
    base = jax.random.normal(key, (D, QW + 2 * KW), jnp.float32) * D ** (-0.5)
    return base.astype(jnp.bfloat16)


def draw_block_mask(key, part):
    global_index = jax.random.randint(jax.random.fold_in(key, 1), (), 0, NBLK)
    picks = jax.random.randint(jax.random.fold_in(key, 2), (NBLK, 2), 0, NBLK)
    row_ids = jnp.arange(NBLK, dtype=jnp.int32)[:, None]
    col_ids = jnp.arange(NBLK, dtype=jnp.int32)[None, :]
    chosen = (jnp.abs(row_ids - col_ids) <= 1) | (col_ids == global_index) | (row_ids == global_index)
    chosen = chosen | (col_ids == picks[:, 0:1]) | (col_ids == picks[:, 1:2])
    return chosen.astype(jnp.int32)


def levels(own_key, shape, cuts, smallest, top_value):
    factor_of = 1.0
    for position, blocks in cuts:
        steps = jax.random.uniform(jax.random.fold_in(jax.random.fold_in(own_key, 6), position), (blocks,), jnp.float32, smallest / len(cuts), top_value / len(cuts))
        factor_of = factor_of * jnp.repeat(jnp.exp(steps), shape[position] // blocks).reshape((-1,) + (1,) * (len(shape) - 1 - position))
    return factor_of


def gaussian(stream_key, extent, deviation, limit, split=(), kind=jnp.bfloat16):
    drawn = deviation * jax.random.normal(stream_key, extent, jnp.float32)
    if split:
        drawn = drawn * levels(stream_key, extent, split, -0.22, 0.18)
    return jnp.clip(drawn, -limit, limit).astype(kind)


def setup_inputs(seed: int = 0) -> dict:
    streams_of = jax.random.split(jax.random.key(seed), 6)
    return {
        "tokens": gaussian(streams_of[0], (BATCH, SEQ, D), 1.0, 6.0, ((0, 8), (1, 16))),
        "norm_gain": jnp.clip(1.0 + 0.18 * jax.random.normal(streams_of[1], (D,), jnp.float32), 0.1, 1.9),
        "qkv_weight": draw_qkv_weight(jax.random.fold_in(streams_of[5], 71), 0),
        "block_mask": draw_block_mask(jax.random.fold_in(streams_of[5], 71), 0),
        "out_grad": gaussian(streams_of[4], (BATCH, SEQ, QW), 1.0, 6.0, ((0, 8), (1, 16))),
    }


epsilon = 1e-05

def reference(tokens, norm_gain, qkv_weight, block_mask, out_grad):
    group_size = HEADS // KV_HEADS
    score_scale = 1.0 / math.sqrt(HEAD_DIM)
    allowed_rows = block_mask == 1

    def one_sequence(seq_pair):
        seq_tokens, seq_grad = seq_pair
        inputs = seq_tokens.astype(jnp.float32)
        inv_rms = lax.rsqrt(lax.optimization_barrier(jnp.mean(inputs * inputs, axis=1, keepdims=True)) + epsilon)
        normed = (inputs * inv_rms * norm_gain).astype(jnp.bfloat16)
        projected = jnp.dot(normed, qkv_weight, preferred_element_type=jnp.float32).astype(jnp.bfloat16)
        queries = projected[:, :QW].astype(jnp.float32).reshape(SEQ, KV_HEADS, group_size, HEAD_DIM)
        key_heads = projected[:, QW:QW + KW].astype(jnp.float32).reshape(SEQ, KV_HEADS, HEAD_DIM)
        values = projected[:, QW + KW:].astype(jnp.float32).reshape(SEQ, KV_HEADS, HEAD_DIM)
        grad_heads = seq_grad.astype(jnp.float32).reshape(SEQ, KV_HEADS, group_size, HEAD_DIM)

        def block_scores(block_index):
            query_block = lax.dynamic_slice_in_dim(queries, block_index * BLOCK, BLOCK, 0)
            scores = jnp.einsum('bkgd,skd->kgbs', query_block, key_heads) * score_scale
            allowed = jnp.repeat(allowed_rows[block_index], BLOCK)[None, None, None, :]
            return (query_block, scores, allowed)

        def forward(block_index):
            query_block, scores, allowed = block_scores(block_index)
            masked = jnp.where(allowed, scores, -jnp.inf)
            row_max = lax.optimization_barrier(jnp.max(masked, axis=-1, keepdims=True))
            exp_weights = jnp.where(allowed, jnp.exp(masked - row_max), 0.0)
            row_total = lax.optimization_barrier(jnp.sum(exp_weights, axis=-1))
            weights = lax.optimization_barrier(exp_weights.astype(jnp.bfloat16)).astype(jnp.float32)
            mixed = jnp.einsum('kgbs,skd->kgbd', weights, values) / row_total[..., None]
            attended = mixed.transpose(2, 0, 1, 3).reshape(BLOCK, QW).astype(jnp.bfloat16)
            return (attended, row_max[..., 0] + jnp.log(row_total))
        attended_blocks, log_blocks = lax.map(forward, jnp.arange(NBLK, dtype=jnp.int32))
        attended = attended_blocks.reshape(SEQ, QW)
        attended_heads = attended.astype(jnp.float32).reshape(SEQ, KV_HEADS, group_size, HEAD_DIM)

        def backward(carried, block_index):
            key_grad, value_grad = carried
            query_block, scores, allowed = block_scores(block_index)
            grad_block = lax.dynamic_slice_in_dim(grad_heads, block_index * BLOCK, BLOCK, 0)
            attended_block = lax.dynamic_slice_in_dim(attended_heads, block_index * BLOCK, BLOCK, 0)
            delta_rows = lax.optimization_barrier(jnp.sum(grad_block * attended_block, axis=-1)).transpose(1, 2, 0)
            prob_full = jnp.where(allowed, jnp.exp(scores - log_blocks[block_index][..., None]), 0.0)
            prob_half = lax.optimization_barrier(prob_full.astype(jnp.bfloat16)).astype(jnp.float32)
            value_grad = value_grad + jnp.einsum('kgbs,bkgd->skd', prob_half, grad_block)
            prob_grad = jnp.einsum('bkgd,skd->kgbs', grad_block, values)
            score_grad = prob_full * (prob_grad - delta_rows[..., None])
            score_half = lax.optimization_barrier(score_grad.astype(jnp.bfloat16)).astype(jnp.float32)
            query_grad = jnp.einsum('kgbs,skd->bkgd', score_half, key_heads) * score_scale
            key_grad = key_grad + jnp.einsum('kgbs,bkgd->skd', score_half, query_block) * score_scale
            return ((key_grad, value_grad), query_grad.reshape(BLOCK, QW))
        zeros_heads = jnp.zeros((SEQ, KV_HEADS, HEAD_DIM), jnp.float32)
        (key_grad, value_grad), query_grad = lax.scan(backward, (zeros_heads, zeros_heads), jnp.arange(NBLK, dtype=jnp.int32))
        projected_grad = jnp.concatenate([query_grad.reshape(SEQ, QW), key_grad.reshape(SEQ, KW), value_grad.reshape(SEQ, KW)], axis=1).astype(jnp.bfloat16)
        normed_grad = jnp.dot(projected_grad, qkv_weight.T, preferred_element_type=jnp.float32)
        scaled = normed_grad * norm_gain
        input_grad = inv_rms * scaled - inputs * inv_rms ** 3 * lax.optimization_barrier(jnp.mean(scaled * inputs, axis=1, keepdims=True))
        return (attended, input_grad.astype(jnp.bfloat16))
    attended, token_grad = lax.map(one_sequence, (tokens, out_grad))
    return (attended, token_grad)
```

```python
import math

import jax
import jax.numpy as jnp
from jax import lax
from jax.experimental import pallas as pl
from jax.experimental.pallas import tpu as pltpu
from jax.sharding import PartitionSpec as P

HEADS = 12
KV_HEADS = 4
HEAD_DIM = 128
BLOCK = 128


epsilon = 1e-05
very_low = -1e30


def attention_kernel(mask_ref, q_ref, do_ref, kv_ref, att_ref, dq_ref, dkv_ref, s_ref, list_ref, count_ref):
    scale = 1.0 / math.sqrt(128)
    position = lax.axis_index("ctx")
    dkv_ref[...] = jnp.zeros_like(dkv_ref)
    for r in range(2):
        def note(j, n):
            list_ref[r, n] = j
            return n + mask_ref[position * 2 + r, j]
        count_ref[r] = lax.fori_loop(0, 32, note, 0)

    def unit(u, carry):
        r, h = u // 4, u % 4
        rows = pl.ds(pl.multiple_of(r * 128, 128), 128)
        cols = [pl.ds(pl.multiple_of(h * 384 + i * 128, 128), 128) for i in range(3)]
        kcol = pl.ds(pl.multiple_of(h * 128, 128), 128)
        vcol = pl.ds(pl.multiple_of(512 + h * 128, 128), 128)
        q = jnp.concatenate([q_ref[rows, c] for c in cols], axis=0)
        do = jnp.concatenate([do_ref[rows, c] for c in cols], axis=0)
        n = count_ref[r]
        pairs = (n + 1) // 2

        def ids(p):
            second = jnp.minimum(2 * p + 1, n - 1)
            return list_ref[r, 2 * p], list_ref[r, second], 2 * p + 1 < n

        def load(p, col):
            a, b, _ = ids(p)
            return jnp.concatenate([kv_ref[pl.ds(pl.multiple_of(a * 128, 128), 128), col],
                                    kv_ref[pl.ds(pl.multiple_of(b * 128, 128), 128), col]], axis=0)

        def score(p, m):
            _, _, valid = ids(p)
            s = lax.dot_general(load(p, kcol), q, (((1,), (1,)), ((), ())), preferred_element_type=jnp.float32) * scale
            low = s[128:]
            low = jnp.where(valid, low, -1e30)
            s_ref[p, :128] = s[:128]
            s_ref[p, 128:] = low
            return jnp.maximum(m, jnp.maximum(jnp.max(s[:128], axis=0, keepdims=True), jnp.max(low, axis=0, keepdims=True)))
        m = lax.fori_loop(0, pairs, score, jnp.full((1, 384), -1e30, jnp.float32))

        def weigh(p, carry):
            total, acc = carry
            _, _, valid = ids(p)
            e = jnp.exp(s_ref[p] - m)
            s_ref[p] = e
            total = total + jnp.sum(e, axis=0, keepdims=True)
            acc = acc + lax.dot_general(load(p, vcol), e.astype(jnp.bfloat16), (((0,), (0,)), ((), ())), preferred_element_type=jnp.float32)
            return total, acc
        total, acc = lax.fori_loop(0, pairs, weigh, (jnp.zeros((1, 384), jnp.float32), jnp.zeros((128, 384), jnp.float32)))
        inverse = 1.0 / total
        out_t = acc * inverse
        out = out_t.T
        for i in range(3):
            att_ref[rows, cols[i]] = out[i * 128:(i + 1) * 128].astype(jnp.bfloat16)
        out_half = out_t.astype(jnp.bfloat16).astype(jnp.float32)
        do_t = do.astype(jnp.float32).T
        delta = jnp.sum(out_half * do_t, axis=0, keepdims=True)

        def back(p, dq_t):
            a, b, valid = ids(p)
            k, v = load(p, kcol), load(p, vcol)
            prob = s_ref[p] * inverse
            dprob = lax.dot_general(v, do, (((1,), (1,)), ((), ())), preferred_element_type=jnp.float32)
            ds = (prob * (dprob - delta)).astype(jnp.bfloat16)
            dv = jnp.dot(prob.astype(jnp.bfloat16), do, preferred_element_type=jnp.float32)
            dk = jnp.dot(ds, q, preferred_element_type=jnp.float32) * scale
            dq_t = dq_t + lax.dot_general(k, ds, (((0,), (0,)), ((), ())), preferred_element_type=jnp.float32)

            def put(block, lo):
                where = pl.ds(pl.multiple_of(block * 128, 128), 128)
                dkv_ref[where, kcol] = (dkv_ref[where, kcol].astype(jnp.float32) + dk[lo:lo + 128]).astype(jnp.bfloat16)
                dkv_ref[where, vcol] = (dkv_ref[where, vcol].astype(jnp.float32) + dv[lo:lo + 128]).astype(jnp.bfloat16)
            put(a, 0)
            pl.when(valid)(lambda: put(b, 128))
            return dq_t
        dq = lax.fori_loop(0, pairs, back, jnp.zeros((128, 384), jnp.float32)).T * scale
        for i in range(3):
            dq_ref[rows, cols[i]] = dq[i * 128:(i + 1) * 128].astype(jnp.bfloat16)
        return carry
    lax.fori_loop(0, 8, unit, 0)

def attention(block_mask, q, do, kv):
    vm = pl.BlockSpec(memory_space=pltpu.VMEM)
    return pl.pallas_call(
        attention_kernel,
        out_shape=(jax.ShapeDtypeStruct((256, 1536), jnp.bfloat16), jax.ShapeDtypeStruct((256, 1536), jnp.bfloat16),
                   jax.ShapeDtypeStruct((4096, 1024), jnp.bfloat16)),
        in_specs=[pl.BlockSpec(memory_space=pltpu.SMEM), vm, vm, vm],
        out_specs=(vm, vm, vm),
        scratch_shapes=[pltpu.VMEM((16, 256, 384), jnp.float32), pltpu.SMEM((2, 33), jnp.int32), pltpu.SMEM((2,), jnp.int32)],
        compiler_params=pltpu.CompilerParams(vmem_limit_bytes=60 << 20),
        name="attention",
    )(block_mask, q, do, kv)


def body(tokens, norm_gain, qkv_weight, block_mask, out_grad):
    rows_here = tokens.shape[1]
    group_size = HEADS // KV_HEADS
    query_width = HEADS * HEAD_DIM
    key_width = KV_HEADS * HEAD_DIM
    score_scale = 1.0 / math.sqrt(HEAD_DIM)
    cycle_size = lax.axis_size("ctx")
    position = lax.axis_index("ctx")
    blocks_here = rows_here // BLOCK
    inputs = tokens[0].astype(jnp.float32)
    inv_rms = lax.rsqrt(jnp.mean(inputs * inputs, axis=1, keepdims=True) + epsilon)
    normed = (inputs * inv_rms * norm_gain).astype(jnp.bfloat16)
    panels = lax.all_gather(qkv_weight, "fsdp", axis=0, tiled=True)
    projected = jnp.dot(normed, panels, preferred_element_type=jnp.float32).astype(jnp.bfloat16)
    pairs_all = lax.all_gather(projected[:, query_width:], "ctx", axis=0, tiled=True)
    attended, query_rows_grad, block_terms = attention(block_mask, projected[:, :query_width], out_grad[0], pairs_all)
    pair_grads = lax.psum_scatter(
        block_terms, "ctx", scatter_dimension=0, tiled=True
    ).astype(jnp.float32)
    projected_grad = jnp.concatenate([query_rows_grad, pair_grads.astype(jnp.bfloat16)], axis=1)
    normed_grad = lax.dot_general(
        projected_grad, panels, (((1,), (1,)), ((), ())), preferred_element_type=jnp.float32
    )
    scaled = normed_grad * norm_gain
    token_grad = inv_rms * scaled - inputs * inv_rms**3 * jnp.mean(
        scaled * inputs, axis=1, keepdims=True
    )
    return (attended[None], token_grad.astype(jnp.bfloat16)[None])


def solution(mesh):
    in_specs = (P("fsdp", "ctx", None), P(), P("fsdp", None), P(), P("fsdp", "ctx", None))
    out_specs = (P("fsdp", "ctx", None), P("fsdp", "ctx", None))
    return jax.shard_map(body, mesh=mesh, in_specs=in_specs, out_specs=out_specs, check_vma=False)
```

```python
import math

import jax
import jax.numpy as jnp
from jax import lax
from jax.experimental import pallas as pl
from jax.experimental.pallas import tpu as pltpu
from jax.sharding import PartitionSpec as P

HEADS = 12
KV_HEADS = 4
HEAD_DIM = 128
BLOCK = 128


epsilon = 1e-05
very_low = -1e30


MESH = pl.DeviceIdType.MESH
D = 3072
KEYS = pl.ds(1536, 1024)
QUERIES = pl.ds(0, 1536)


class Place:
    def __init__(self):
        self.i = lax.axis_index("ctx")
        self.f = lax.axis_index("fsdp")
        self.c = self.i % 2
        self.y = (self.i // 2) % 4
        self.z = (self.i // 8) * 2 + self.f // 4
        self.x = self.f % 4

    def ids(self, dx=0, dy=0, dz=0, swap=False):
        x, y, z = (self.x + dx) % 4, (self.y + dy) % 4, (self.z + dz) % 4
        c = 1 - self.c if swap else self.c
        return ((z // 2) * 4 + y) * 2 + c, (z % 2) * 4 + x


class Net:
    def __init__(self, send_sem, recv_sem):
        self.send_sem, self.recv_sem, self.copies = send_sem, recv_sem, {}

    def send(self, name, src, dst, to):
        k = len(self.copies)
        copy = pltpu.make_async_remote_copy(
            src_ref=src, dst_ref=dst, send_sem=self.send_sem.at[k], recv_sem=self.recv_sem.at[k],
            device_id=to, device_id_type=MESH)
        copy.start()
        self.copies[name] = copy

    def recv(self, name):
        self.copies[name].wait_recv()

    def drain(self):
        for copy in self.copies.values():
            copy.wait_send()


def greet(place):
    barrier = pltpu.get_barrier_semaphore()
    peers = [place.ids(dx=1), place.ids(dx=-1), place.ids(dy=1), place.ids(dy=-1),
             place.ids(dz=1), place.ids(dz=-1), place.ids(swap=True)]
    for peer in peers:
        pl.semaphore_signal(barrier, inc=1, device_id=peer, device_id_type=MESH)
    pl.semaphore_wait(barrier, len(peers))


def rows_at(start, count):
    return pl.ds(pl.multiple_of(start, 32), count)


class WeightGather:
    def __init__(self, net, place, tag, shard, whole, cols):
        self.net, self.p, self.tag, self.shard, self.whole, self.cols = net, place, tag, shard, whole, cols

    def at(self, dx, lo, count):
        shard_id = (self.p.f // 4) * 4 + (self.p.x + dx) % 4
        return self.whole.at[rows_at(shard_id * 384 + self.p.c * 192 + lo, count), self.cols]

    def own(self, lo, count):
        return self.shard.at[rows_at(self.p.c * 192 + lo, count), self.cols]

    def cross(self, dx, lo):
        shard_id = (1 - self.p.f // 4) * 4 + (self.p.x + dx) % 4
        return self.whole.at[rows_at(shard_id * 384 + self.p.c * 192 + lo, 96), self.cols]

    def put(self, name, piece, to, src=None):
        self.net.send(self.tag + name, piece if src is None else src, piece, to)

    def start_x(self):
        self.put("x+", self.at(0, 0, 192), self.p.ids(dx=1), self.own(0, 192))
        self.put("x-", self.at(0, 0, 192), self.p.ids(dx=-1), self.own(0, 192))

    def start_z(self):
        self.put("z+0", self.at(0, 0, 96), self.p.ids(dz=1), self.own(0, 96))
        self.put("z-0", self.at(0, 96, 96), self.p.ids(dz=-1), self.own(96, 96))

    def got(self, name):
        self.net.recv(self.tag + name)

    def first(self):
        self.got("x+")
        self.put("x+2", self.at(-1, 0, 96), self.p.ids(dx=1))
        self.got("x-")
        self.put("x-2", self.at(1, 96, 96), self.p.ids(dx=-1))
        for dx in (-1, 1):
            self.put("z+%d" % dx, self.at(dx, 0, 96), self.p.ids(dz=1))
            self.put("z-%d" % dx, self.at(dx, 96, 96), self.p.ids(dz=-1))
            self.put("c%d" % dx, self.at(dx, 0, 192), self.p.ids(swap=True))

    def second(self):
        for sign, lo, dz in (("+", 0, 1), ("-", 96, -1)):
            self.got("x%s2" % sign)
            self.put("z%s2" % sign, self.at(2, lo, 96), self.p.ids(dz=dz))
            self.put("c2%s" % sign, self.at(2, lo, 96), self.p.ids(swap=True))

    def third(self):
        for dx in (0, -1, 1, 2):
            for sign, lo in (("+", 0), ("-", 96)):
                self.got("z%s%d" % (sign, dx))
                self.put("cz%s%d" % (sign, dx), self.cross(dx, lo), self.p.ids(swap=True))

    def last(self):
        for name in ("c-1", "c1", "c2+", "c2-"):
            self.got(name)
        for dx in (0, -1, 1, 2):
            for sign in "+-":
                self.got("cz%s%d" % (sign, dx))


def project_kernel(tok_ref, gain_ref, shard, q_ref, kv_all, w_all, w_vm, normed, kv_own, relay, send_sem, recv_sem,
                   local_sem):
    p = Place()
    net = Net(send_sem, recv_sem)
    greet(p)
    keys = WeightGather(net, p, "k", shard, w_vm, KEYS)
    queries = WeightGather(net, p, "q", shard, w_vm, QUERIES)
    keys.start_x()
    keys.start_z()
    mine = pltpu.make_async_copy(shard, w_vm.at[rows_at(p.f * 384, 384)], local_sem.at[0])
    mine.start()

    @pl.loop(0, 8)
    def _(t):
        rows = pl.ds(pl.multiple_of(t * 32, 32), 32)
        x = tok_ref[rows, :].astype(jnp.float32)
        inv_rms = lax.rsqrt(jnp.mean(x * x, axis=1, keepdims=True) + epsilon)
        normed[rows, :] = (x * inv_rms * gain_ref[...]).astype(jnp.bfloat16)

    keys.first()
    queries.start_x()
    keys.second()
    queries.start_z()
    keys.third()
    keys.last()
    mine.wait()

    @pl.loop(0, 4)
    def _(t):
        cols = pl.ds(pl.multiple_of(t * 256, 256), 256)
        part = jnp.dot(normed[...], w_vm[:, pl.ds(pl.multiple_of(1536 + t * 256, 256), 256)],
                       preferred_element_type=jnp.float32)
        kv_own[:, cols] = part.astype(jnp.bfloat16)

    keep_keys = pltpu.make_async_copy(w_vm.at[:, KEYS], w_all.at[:, KEYS], local_sem.at[1])
    keep_keys.start()

    def home(dy=0, dz=0, lo=0, count=256):
        who, _ = p.ids(dy=dy, dz=dz)
        return kv_all.at[rows_at(who * 256 + lo, count)]

    def put(name, piece, to, src=None):
        net.send(name, piece if src is None else src, piece, to)

    swap, up, down, north, south = p.ids(swap=True), p.ids(dz=1), p.ids(dz=-1), p.ids(dy=1), p.ids(dy=-1)
    put("y+", home(), north, kv_own)
    put("y-", home(), south, kv_own)
    put("h+", relay.at[0], up, kv_own.at[:128])
    put("h-", relay.at[1], down, kv_own.at[128:])
    put("cy0", home(), swap, kv_own)
    stay = pltpu.make_async_copy(kv_own, home(), local_sem.at[2])
    stay.start()

    queries.first()
    net.recv("h+")
    put("r+", home(dz=-1, count=128), up, relay.at[0])
    net.recv("h-")
    put("r-", home(dz=1, lo=128, count=128), down, relay.at[1])
    queries.second()
    for sign, lo in (("+", 0), ("-", 128)):
        net.recv("r" + sign)
        piece = home(dz=2, lo=lo, count=128)
        put("ty+" + sign, piece, north)
        put("ty-" + sign, piece, south)
        put("ct" + sign, piece, swap)
    net.recv("y+")
    put("y+2", home(dy=-1, count=128), north)
    put("cy-", home(dy=-1), swap)
    net.recv("y-")
    put("y-2", home(dy=1, lo=128, count=128), south)
    put("cy+", home(dy=1), swap)
    queries.third()
    queries.last()

    keep_queries = pltpu.make_async_copy(w_vm.at[:, QUERIES], w_all.at[:, QUERIES], local_sem.at[3])
    keep_queries.start()

    net.recv("ty++")
    put("ty+2", home(dy=-1, dz=2, count=128), north)
    put("ct-a", home(dy=-1, dz=2, count=128), swap)
    net.recv("ty--")
    put("ty-2", home(dy=1, dz=2, lo=128, count=128), south)
    put("ct+b", home(dy=1, dz=2, lo=128, count=128), swap)
    net.recv("ty+-")
    put("ct-b", home(dy=-1, dz=2, lo=128, count=128), swap)
    net.recv("ty-+")
    put("ct+a", home(dy=1, dz=2, count=128), swap)

    @pl.loop(0, 6)
    def _(t):
        cols = pl.ds(pl.multiple_of(t * 256, 256), 256)
        q_ref[:, cols] = jnp.dot(normed[...], w_vm[:, cols], preferred_element_type=jnp.float32).astype(jnp.bfloat16)

    net.recv("y+2")
    put("cy2a", home(dy=2, count=128), swap)
    net.recv("y-2")
    put("cy2b", home(dy=2, lo=128, count=128), swap)
    net.recv("ty+2")
    put("ct2a", home(dy=2, dz=2, count=128), swap)
    net.recv("ty-2")
    put("ct2b", home(dy=2, dz=2, lo=128, count=128), swap)
    for name in ("cy0", "cy-", "cy+", "cy2a", "cy2b", "ct+", "ct-", "ct-a", "ct+b", "ct-b", "ct+a", "ct2a", "ct2b"):
        net.recv(name)
    net.drain()
    for copy in (stay, keep_keys, keep_queries):
        copy.wait()


def project(tokens, gain, shard):
    vm, anywhere = pl.BlockSpec(memory_space=pltpu.VMEM), pl.BlockSpec(memory_space=pl.ANY)
    half = jnp.bfloat16
    return pl.pallas_call(
        project_kernel,
        out_shape=(jax.ShapeDtypeStruct((256, 1536), half), jax.ShapeDtypeStruct((4096, 1024), half),
                   jax.ShapeDtypeStruct((3072, 2560), half)),
        in_specs=[vm, vm, anywhere],
        out_specs=(vm, anywhere, anywhere),
        scratch_shapes=[pltpu.VMEM((3072, 2560), half), pltpu.VMEM((256, 3072), half), pltpu.VMEM((256, 1024), half),
                        pltpu.VMEM((2, 128, 1024), half), pltpu.SemaphoreType.DMA((80,)),
                        pltpu.SemaphoreType.DMA((80,)), pltpu.SemaphoreType.DMA((4,))],
        compiler_params=pltpu.CompilerParams(vmem_limit_bytes=60 << 20, collective_id=0, has_side_effects=True),
        name="project",
    )(tokens, gain, shard)


def attention_kernel(mask_ref, q_ref, do_ref, kv_ref, att_ref, dq_ref, dkv_ref, s_ref, list_ref, count_ref):
    scale = 1.0 / math.sqrt(128)
    position = lax.axis_index("ctx")
    dkv_ref[...] = jnp.zeros_like(dkv_ref)
    for r in range(2):
        def note(j, n):
            list_ref[r, n] = j
            return n + mask_ref[position * 2 + r, j]
        count_ref[r] = lax.fori_loop(0, 32, note, 0)

    def unit(u, carry):
        r, h = u // 4, u % 4
        rows = pl.ds(pl.multiple_of(r * 128, 128), 128)
        cols = [pl.ds(pl.multiple_of(h * 384 + i * 128, 128), 128) for i in range(3)]
        kcol = pl.ds(pl.multiple_of(h * 128, 128), 128)
        vcol = pl.ds(pl.multiple_of(512 + h * 128, 128), 128)
        q = jnp.concatenate([q_ref[rows, c] for c in cols], axis=0)
        do = jnp.concatenate([do_ref[rows, c] for c in cols], axis=0)
        n = count_ref[r]
        pairs = (n + 1) // 2

        def ids(p):
            second = jnp.minimum(2 * p + 1, n - 1)
            return list_ref[r, 2 * p], list_ref[r, second], 2 * p + 1 < n

        def load(p, col):
            a, b, _ = ids(p)
            return jnp.concatenate([kv_ref[pl.ds(pl.multiple_of(a * 128, 128), 128), col],
                                    kv_ref[pl.ds(pl.multiple_of(b * 128, 128), 128), col]], axis=0)

        def score(p, m):
            _, _, valid = ids(p)
            s = lax.dot_general(load(p, kcol), q, (((1,), (1,)), ((), ())), preferred_element_type=jnp.float32) * scale
            low = s[128:]
            low = jnp.where(valid, low, -1e30)
            s_ref[p, :128] = s[:128]
            s_ref[p, 128:] = low
            return jnp.maximum(m, jnp.maximum(jnp.max(s[:128], axis=0, keepdims=True), jnp.max(low, axis=0, keepdims=True)))
        m = lax.fori_loop(0, pairs, score, jnp.full((1, 384), -1e30, jnp.float32))

        def weigh(p, carry):
            total, acc = carry
            _, _, valid = ids(p)
            e = jnp.exp(s_ref[p] - m)
            s_ref[p] = e
            total = total + jnp.sum(e, axis=0, keepdims=True)
            acc = acc + lax.dot_general(load(p, vcol), e.astype(jnp.bfloat16), (((0,), (0,)), ((), ())), preferred_element_type=jnp.float32)
            return total, acc
        total, acc = lax.fori_loop(0, pairs, weigh, (jnp.zeros((1, 384), jnp.float32), jnp.zeros((128, 384), jnp.float32)))
        inverse = 1.0 / total
        out_t = acc * inverse
        out = out_t.T
        for i in range(3):
            att_ref[rows, cols[i]] = out[i * 128:(i + 1) * 128].astype(jnp.bfloat16)
        out_half = out_t.astype(jnp.bfloat16).astype(jnp.float32)
        do_t = do.astype(jnp.float32).T
        delta = jnp.sum(out_half * do_t, axis=0, keepdims=True)

        def back(p, dq_t):
            a, b, valid = ids(p)
            k, v = load(p, kcol), load(p, vcol)
            prob = s_ref[p] * inverse
            dprob = lax.dot_general(v, do, (((1,), (1,)), ((), ())), preferred_element_type=jnp.float32)
            ds = (prob * (dprob - delta)).astype(jnp.bfloat16)
            dv = jnp.dot(prob.astype(jnp.bfloat16), do, preferred_element_type=jnp.float32)
            dk = jnp.dot(ds, q, preferred_element_type=jnp.float32) * scale
            dq_t = dq_t + lax.dot_general(k, ds, (((0,), (0,)), ((), ())), preferred_element_type=jnp.float32)

            def put(block, lo):
                where = pl.ds(pl.multiple_of(block * 128, 128), 128)
                dkv_ref[where, kcol] = (dkv_ref[where, kcol].astype(jnp.float32) + dk[lo:lo + 128]).astype(jnp.bfloat16)
                dkv_ref[where, vcol] = (dkv_ref[where, vcol].astype(jnp.float32) + dv[lo:lo + 128]).astype(jnp.bfloat16)
            put(a, 0)
            pl.when(valid)(lambda: put(b, 128))
            return dq_t
        dq = lax.fori_loop(0, pairs, back, jnp.zeros((128, 384), jnp.float32)).T * scale
        for i in range(3):
            dq_ref[rows, cols[i]] = dq[i * 128:(i + 1) * 128].astype(jnp.bfloat16)
        return carry
    lax.fori_loop(0, 8, unit, 0)

def attention(block_mask, q, do, kv):
    vm = pl.BlockSpec(memory_space=pltpu.VMEM)
    return pl.pallas_call(
        attention_kernel,
        out_shape=(jax.ShapeDtypeStruct((256, 1536), jnp.bfloat16), jax.ShapeDtypeStruct((256, 1536), jnp.bfloat16),
                   jax.ShapeDtypeStruct((4096, 1024), jnp.bfloat16)),
        in_specs=[pl.BlockSpec(memory_space=pltpu.SMEM), vm, vm, vm],
        out_specs=(vm, vm, vm),
        scratch_shapes=[pltpu.VMEM((16, 256, 384), jnp.float32), pltpu.SMEM((2, 33), jnp.int32), pltpu.SMEM((2,), jnp.int32)],
        compiler_params=pltpu.CompilerParams(vmem_limit_bytes=60 << 20),
        name="attention",
    )(block_mask, q, do, kv)


def body(tokens, norm_gain, qkv_weight, block_mask, out_grad):
    rows_here = tokens.shape[1]
    group_size = HEADS // KV_HEADS
    query_width = HEADS * HEAD_DIM
    key_width = KV_HEADS * HEAD_DIM
    score_scale = 1.0 / math.sqrt(HEAD_DIM)
    cycle_size = lax.axis_size("ctx")
    position = lax.axis_index("ctx")
    blocks_here = rows_here // BLOCK
    inputs = tokens[0].astype(jnp.float32)
    inv_rms = lax.rsqrt(jnp.mean(inputs * inputs, axis=1, keepdims=True) + epsilon)
    queries, pairs_all, panels = project(tokens[0], norm_gain[None], qkv_weight)
    attended, query_rows_grad, block_terms = attention(block_mask, queries, out_grad[0], pairs_all)
    pair_grads = lax.psum_scatter(
        block_terms, "ctx", scatter_dimension=0, tiled=True
    ).astype(jnp.float32)
    projected_grad = jnp.concatenate([query_rows_grad, pair_grads.astype(jnp.bfloat16)], axis=1)
    normed_grad = lax.dot_general(
        projected_grad, panels, (((1,), (1,)), ((), ())), preferred_element_type=jnp.float32
    )
    scaled = normed_grad * norm_gain
    token_grad = inv_rms * scaled - inputs * inv_rms**3 * jnp.mean(
        scaled * inputs, axis=1, keepdims=True
    )
    return (attended[None], token_grad.astype(jnp.bfloat16)[None])


def solution(mesh):
    in_specs = (P("fsdp", "ctx", None), P(), P("fsdp", None), P(), P("fsdp", "ctx", None))
    out_specs = (P("fsdp", "ctx", None), P("fsdp", "ctx", None))
    return jax.shard_map(body, mesh=mesh, in_specs=in_specs, out_specs=out_specs, check_vma=False)
```

```python
import math

import jax
import jax.numpy as jnp
from jax import lax
from jax.experimental import pallas as pl
from jax.experimental.pallas import tpu as pltpu
from jax.sharding import PartitionSpec as P

HEADS = 12
KV_HEADS = 4
HEAD_DIM = 128
BLOCK = 128


epsilon = 1e-05
very_low = -1e30


MESH = pl.DeviceIdType.MESH
D = 3072
KEYS = pl.ds(1536, 1024)
QUERIES = pl.ds(0, 1536)


class Place:
    def __init__(self):
        self.i = lax.axis_index("ctx")
        self.f = lax.axis_index("fsdp")
        self.c = self.i % 2
        self.y = (self.i // 2) % 4
        self.z = (self.i // 8) * 2 + self.f // 4
        self.x = self.f % 4

    def ids(self, dx=0, dy=0, dz=0, swap=False):
        x, y, z = (self.x + dx) % 4, (self.y + dy) % 4, (self.z + dz) % 4
        c = 1 - self.c if swap else self.c
        return ((z // 2) * 4 + y) * 2 + c, (z % 2) * 4 + x


class Net:
    def __init__(self, send_sem, recv_sem):
        self.send_sem, self.recv_sem, self.copies = send_sem, recv_sem, {}

    def send(self, name, src, dst, to):
        k = len(self.copies)
        copy = pltpu.make_async_remote_copy(
            src_ref=src, dst_ref=dst, send_sem=self.send_sem.at[k], recv_sem=self.recv_sem.at[k],
            device_id=to, device_id_type=MESH)
        copy.start()
        self.copies[name] = copy

    def recv(self, name):
        self.copies[name].wait_recv()

    def drain(self):
        for copy in self.copies.values():
            copy.wait_send()


def greet(place):
    barrier = pltpu.get_barrier_semaphore()
    peers = [place.ids(dx=1), place.ids(dx=-1), place.ids(dy=1), place.ids(dy=-1),
             place.ids(dz=1), place.ids(dz=-1), place.ids(swap=True)]
    for peer in peers:
        pl.semaphore_signal(barrier, inc=1, device_id=peer, device_id_type=MESH)
    pl.semaphore_wait(barrier, len(peers))


def rows_at(start, count):
    return pl.ds(pl.multiple_of(start, 32), count)


class WeightGather:
    def __init__(self, net, place, tag, shard, whole, cols):
        self.net, self.p, self.tag, self.shard, self.whole, self.cols = net, place, tag, shard, whole, cols

    def at(self, dx, lo, count):
        shard_id = (self.p.f // 4) * 4 + (self.p.x + dx) % 4
        return self.whole.at[rows_at(shard_id * 384 + self.p.c * 192 + lo, count), self.cols]

    def own(self, lo, count):
        return self.shard.at[rows_at(self.p.c * 192 + lo, count), self.cols]

    def cross(self, dx, lo):
        shard_id = (1 - self.p.f // 4) * 4 + (self.p.x + dx) % 4
        return self.whole.at[rows_at(shard_id * 384 + self.p.c * 192 + lo, 96), self.cols]

    def put(self, name, piece, to, src=None):
        self.net.send(self.tag + name, piece if src is None else src, piece, to)

    def start_x(self):
        self.put("x+", self.at(0, 0, 192), self.p.ids(dx=1), self.own(0, 192))
        self.put("x-", self.at(0, 0, 192), self.p.ids(dx=-1), self.own(0, 192))

    def start_z(self):
        self.put("z+0", self.at(0, 0, 96), self.p.ids(dz=1), self.own(0, 96))
        self.put("z-0", self.at(0, 96, 96), self.p.ids(dz=-1), self.own(96, 96))

    def got(self, name):
        self.net.recv(self.tag + name)

    def first(self):
        self.got("x+")
        self.put("x+2", self.at(-1, 0, 96), self.p.ids(dx=1))
        self.got("x-")
        self.put("x-2", self.at(1, 96, 96), self.p.ids(dx=-1))
        for dx in (-1, 1):
            self.put("z+%d" % dx, self.at(dx, 0, 96), self.p.ids(dz=1))
            self.put("z-%d" % dx, self.at(dx, 96, 96), self.p.ids(dz=-1))
            self.put("c%d" % dx, self.at(dx, 0, 192), self.p.ids(swap=True))

    def second(self):
        for sign, lo, dz in (("+", 0, 1), ("-", 96, -1)):
            self.got("x%s2" % sign)
            self.put("z%s2" % sign, self.at(2, lo, 96), self.p.ids(dz=dz))
            self.put("c2%s" % sign, self.at(2, lo, 96), self.p.ids(swap=True))

    def third(self):
        for dx in (0, -1, 1, 2):
            for sign, lo in (("+", 0), ("-", 96)):
                self.got("z%s%d" % (sign, dx))
                self.put("cz%s%d" % (sign, dx), self.cross(dx, lo), self.p.ids(swap=True))

    def last(self):
        for name in ("c-1", "c1", "c2+", "c2-"):
            self.got(name)
        for dx in (0, -1, 1, 2):
            for sign in "+-":
                self.got("cz%s%d" % (sign, dx))


def project_kernel(tok_ref, gain_ref, shard, q_ref, kv_all, w_all, w_vm, normed, kv_own, relay, send_sem, recv_sem,
                   local_sem):
    p = Place()
    net = Net(send_sem, recv_sem)
    greet(p)
    keys = WeightGather(net, p, "k", shard, w_vm, KEYS)
    queries = WeightGather(net, p, "q", shard, w_vm, QUERIES)
    keys.start_x()
    keys.start_z()
    mine = pltpu.make_async_copy(shard, w_vm.at[rows_at(p.f * 384, 384)], local_sem.at[0])
    mine.start()

    @pl.loop(0, 8)
    def _(t):
        rows = pl.ds(pl.multiple_of(t * 32, 32), 32)
        x = tok_ref[rows, :].astype(jnp.float32)
        inv_rms = lax.rsqrt(jnp.mean(x * x, axis=1, keepdims=True) + epsilon)
        normed[rows, :] = (x * inv_rms * gain_ref[...]).astype(jnp.bfloat16)

    keys.first()
    queries.start_x()
    keys.second()
    queries.start_z()
    keys.third()
    keys.last()
    mine.wait()

    @pl.loop(0, 4)
    def _(t):
        cols = pl.ds(pl.multiple_of(t * 256, 256), 256)
        part = jnp.dot(normed[...], w_vm[:, pl.ds(pl.multiple_of(1536 + t * 256, 256), 256)],
                       preferred_element_type=jnp.float32)
        kv_own[:, cols] = part.astype(jnp.bfloat16)

    keep_keys = pltpu.make_async_copy(w_vm.at[:, KEYS], w_all.at[:, KEYS], local_sem.at[1])
    keep_keys.start()

    def home(dy=0, dz=0, lo=0, count=256):
        who, _ = p.ids(dy=dy, dz=dz)
        return kv_all.at[rows_at(who * 256 + lo, count)]

    def put(name, piece, to, src=None):
        net.send(name, piece if src is None else src, piece, to)

    swap, up, down, north, south = p.ids(swap=True), p.ids(dz=1), p.ids(dz=-1), p.ids(dy=1), p.ids(dy=-1)
    put("y+", home(), north, kv_own)
    put("y-", home(), south, kv_own)
    put("h+", relay.at[0], up, kv_own.at[:128])
    put("h-", relay.at[1], down, kv_own.at[128:])
    put("cy0", home(), swap, kv_own)
    stay = pltpu.make_async_copy(kv_own, home(), local_sem.at[2])
    stay.start()

    queries.first()
    net.recv("h+")
    put("r+", home(dz=-1, count=128), up, relay.at[0])
    net.recv("h-")
    put("r-", home(dz=1, lo=128, count=128), down, relay.at[1])
    queries.second()
    for sign, lo in (("+", 0), ("-", 128)):
        net.recv("r" + sign)
        piece = home(dz=2, lo=lo, count=128)
        put("ty+" + sign, piece, north)
        put("ty-" + sign, piece, south)
        put("ct" + sign, piece, swap)
    net.recv("y+")
    put("y+2", home(dy=-1, count=128), north)
    put("cy-", home(dy=-1), swap)
    net.recv("y-")
    put("y-2", home(dy=1, lo=128, count=128), south)
    put("cy+", home(dy=1), swap)
    queries.third()
    queries.last()

    keep_queries = pltpu.make_async_copy(w_vm.at[:, QUERIES], w_all.at[:, QUERIES], local_sem.at[3])
    keep_queries.start()

    net.recv("ty++")
    put("ty+2", home(dy=-1, dz=2, count=128), north)
    put("ct-a", home(dy=-1, dz=2, count=128), swap)
    net.recv("ty--")
    put("ty-2", home(dy=1, dz=2, lo=128, count=128), south)
    put("ct+b", home(dy=1, dz=2, lo=128, count=128), swap)
    net.recv("ty+-")
    put("ct-b", home(dy=-1, dz=2, lo=128, count=128), swap)
    net.recv("ty-+")
    put("ct+a", home(dy=1, dz=2, count=128), swap)

    @pl.loop(0, 6)
    def _(t):
        cols = pl.ds(pl.multiple_of(t * 256, 256), 256)
        q_ref[:, cols] = jnp.dot(normed[...], w_vm[:, cols], preferred_element_type=jnp.float32).astype(jnp.bfloat16)

    net.recv("y+2")
    put("cy2a", home(dy=2, count=128), swap)
    net.recv("y-2")
    put("cy2b", home(dy=2, lo=128, count=128), swap)
    net.recv("ty+2")
    put("ct2a", home(dy=2, dz=2, count=128), swap)
    net.recv("ty-2")
    put("ct2b", home(dy=2, dz=2, lo=128, count=128), swap)
    for name in ("cy0", "cy-", "cy+", "cy2a", "cy2b", "ct+", "ct-", "ct-a", "ct+b", "ct-b", "ct+a", "ct2a", "ct2b"):
        net.recv(name)
    net.drain()
    for copy in (stay, keep_keys, keep_queries):
        copy.wait()


def project(tokens, gain, shard):
    vm, anywhere = pl.BlockSpec(memory_space=pltpu.VMEM), pl.BlockSpec(memory_space=pl.ANY)
    half = jnp.bfloat16
    return pl.pallas_call(
        project_kernel,
        out_shape=(jax.ShapeDtypeStruct((256, 1536), half), jax.ShapeDtypeStruct((4096, 1024), half),
                   jax.ShapeDtypeStruct((3072, 2560), half)),
        in_specs=[vm, vm, anywhere],
        out_specs=(vm, anywhere, anywhere),
        scratch_shapes=[pltpu.VMEM((3072, 2560), half), pltpu.VMEM((256, 3072), half), pltpu.VMEM((256, 1024), half),
                        pltpu.VMEM((2, 128, 1024), half), pltpu.SemaphoreType.DMA((80,)),
                        pltpu.SemaphoreType.DMA((80,)), pltpu.SemaphoreType.DMA((4,))],
        compiler_params=pltpu.CompilerParams(vmem_limit_bytes=60 << 20, collective_id=0, has_side_effects=True),
        name="project",
    )(tokens, gain, shard)


def attention_kernel(mask_ref, q_ref, do_ref, kv_ref, att_ref, dq_ref, dkv_ref, s_ref, list_ref, count_ref):
    scale = 1.0 / math.sqrt(128)
    position = lax.axis_index("ctx")
    dkv_ref[...] = jnp.zeros_like(dkv_ref)
    for r in range(2):
        def note(j, n):
            list_ref[r, n] = j
            return n + mask_ref[position * 2 + r, j]
        count_ref[r] = lax.fori_loop(0, 32, note, 0)

    def unit(u, carry):
        r, h = u // 4, u % 4
        rows = pl.ds(pl.multiple_of(r * 128, 128), 128)
        cols = [pl.ds(pl.multiple_of(h * 384 + i * 128, 128), 128) for i in range(3)]
        kcol = pl.ds(pl.multiple_of(h * 128, 128), 128)
        vcol = pl.ds(pl.multiple_of(512 + h * 128, 128), 128)
        q = jnp.concatenate([q_ref[rows, c] for c in cols], axis=0)
        do = jnp.concatenate([do_ref[rows, c] for c in cols], axis=0)
        n = count_ref[r]
        pairs = (n + 1) // 2

        def ids(p):
            second = jnp.minimum(2 * p + 1, n - 1)
            return list_ref[r, 2 * p], list_ref[r, second], 2 * p + 1 < n

        def load(p, col):
            a, b, _ = ids(p)
            return jnp.concatenate([kv_ref[pl.ds(pl.multiple_of(a * 128, 128), 128), col],
                                    kv_ref[pl.ds(pl.multiple_of(b * 128, 128), 128), col]], axis=0)

        def score(p, m):
            _, _, valid = ids(p)
            s = lax.dot_general(load(p, kcol), q, (((1,), (1,)), ((), ())), preferred_element_type=jnp.float32) * scale
            low = s[128:]
            low = jnp.where(valid, low, -1e30)
            s_ref[p, :128] = s[:128]
            s_ref[p, 128:] = low
            return jnp.maximum(m, jnp.maximum(jnp.max(s[:128], axis=0, keepdims=True), jnp.max(low, axis=0, keepdims=True)))
        m = lax.fori_loop(0, pairs, score, jnp.full((1, 384), -1e30, jnp.float32))

        def weigh(p, carry):
            total, acc = carry
            _, _, valid = ids(p)
            e = jnp.exp(s_ref[p] - m)
            s_ref[p] = e
            total = total + jnp.sum(e, axis=0, keepdims=True)
            acc = acc + lax.dot_general(load(p, vcol), e.astype(jnp.bfloat16), (((0,), (0,)), ((), ())), preferred_element_type=jnp.float32)
            return total, acc
        total, acc = lax.fori_loop(0, pairs, weigh, (jnp.zeros((1, 384), jnp.float32), jnp.zeros((128, 384), jnp.float32)))
        inverse = 1.0 / total
        out_t = acc * inverse
        out = out_t.T
        for i in range(3):
            att_ref[rows, cols[i]] = out[i * 128:(i + 1) * 128].astype(jnp.bfloat16)
        out_half = out_t.astype(jnp.bfloat16).astype(jnp.float32)
        do_t = do.astype(jnp.float32).T
        delta = jnp.sum(out_half * do_t, axis=0, keepdims=True)

        def back(p, dq_t):
            a, b, valid = ids(p)
            k, v = load(p, kcol), load(p, vcol)
            prob = s_ref[p] * inverse
            dprob = lax.dot_general(v, do, (((1,), (1,)), ((), ())), preferred_element_type=jnp.float32)
            ds = (prob * (dprob - delta)).astype(jnp.bfloat16)
            dv = jnp.dot(prob.astype(jnp.bfloat16), do, preferred_element_type=jnp.float32)
            dk = jnp.dot(ds, q, preferred_element_type=jnp.float32) * scale
            dq_t = dq_t + lax.dot_general(k, ds, (((0,), (0,)), ((), ())), preferred_element_type=jnp.float32)

            def put(block, lo):
                where = pl.ds(pl.multiple_of(block * 128, 128), 128)
                dkv_ref[where, kcol] = (dkv_ref[where, kcol].astype(jnp.float32) + dk[lo:lo + 128]).astype(jnp.bfloat16)
                dkv_ref[where, vcol] = (dkv_ref[where, vcol].astype(jnp.float32) + dv[lo:lo + 128]).astype(jnp.bfloat16)
            put(a, 0)
            pl.when(valid)(lambda: put(b, 128))
            return dq_t
        dq = lax.fori_loop(0, pairs, back, jnp.zeros((128, 384), jnp.float32)).T * scale
        for i in range(3):
            dq_ref[rows, cols[i]] = dq[i * 128:(i + 1) * 128].astype(jnp.bfloat16)
        return carry
    lax.fori_loop(0, 8, unit, 0)

def attention(block_mask, q, do, kv):
    vm = pl.BlockSpec(memory_space=pltpu.VMEM)
    return pl.pallas_call(
        attention_kernel,
        out_shape=(jax.ShapeDtypeStruct((256, 1536), jnp.bfloat16), jax.ShapeDtypeStruct((256, 1536), jnp.bfloat16),
                   jax.ShapeDtypeStruct((4096, 1024), jnp.bfloat16)),
        in_specs=[pl.BlockSpec(memory_space=pltpu.SMEM), vm, vm, vm],
        out_specs=(vm, vm, vm),
        scratch_shapes=[pltpu.VMEM((16, 256, 384), jnp.float32), pltpu.SMEM((2, 33), jnp.int32), pltpu.SMEM((2,), jnp.int32)],
        compiler_params=pltpu.CompilerParams(vmem_limit_bytes=60 << 20),
        name="attention",
    )(block_mask, q, do, kv)


def grads_kernel(tok_ref, gain_ref, dq_ref, terms, w_all, out_ref, w_vm, mine, part, ahead, behind, after, before,
                 relay, crossed, total, send_sem, recv_sem, local_sem):
    p = Place()
    net = Net(send_sem, recv_sem)
    greet(p)
    order = [(dz, dy) for dz in (2, 0) for dy in (2, 1, 3, 0)]
    swap, up, down, north, south = p.ids(swap=True), p.ids(dz=1), p.ids(dz=-1), p.ids(dy=1), p.ids(dy=-1)
    loads = {}
    for slot, (dz, dy) in enumerate(order):
        who, _ = p.ids(dy=dy, dz=dz)
        other, _ = p.ids(dy=dy, dz=dz, swap=True)
        net.send("c%d" % slot, terms.at[rows_at(other * 256, 256)], part.at[slot], swap)
        loads[slot] = pltpu.make_async_copy(terms.at[rows_at(who * 256, 256)], mine.at[slot], local_sem.at[slot])
        loads[slot].start()
    weight = pltpu.make_async_copy(w_all, w_vm, local_sem.at[8])
    weight.start()

    def add(dst, *srcs):
        @pl.loop(0, dst.shape[0] // 64)
        def _(t):
            rows = pl.ds(pl.multiple_of(t * 64, 64), 64)
            value = dst[rows, :]
            for src in srcs:
                value = value + src[rows, :]
            dst[rows, :] = value

    def pair(slot):
        loads[slot].wait()
        net.recv("c%d" % slot)
        add(mine.at[slot], part.at[slot])

    def far(base, plane):
        pair(base)
        net.send("a%d" % plane, mine.at[base, :128], ahead.at[plane], north)
        net.send("b%d" % plane, mine.at[base, 128:], behind.at[plane], south)
        pair(base + 1)
        pair(base + 2)

    def near(base, plane):
        net.recv("a%d" % plane)
        add(mine.at[base + 1, :128], ahead.at[plane])
        net.send("f%d" % plane, mine.at[base + 1], after.at[plane], north)
        net.recv("b%d" % plane)
        add(mine.at[base + 2, 128:], behind.at[plane])
        net.send("g%d" % plane, mine.at[base + 2], before.at[plane], south)
        pair(base + 3)

    def gathered(base, plane):
        net.recv("f%d" % plane)
        net.recv("g%d" % plane)
        add(mine.at[base + 3], after.at[plane], before.at[plane])

    def query_part(first, last):
        @pl.loop(first, last)
        def _(t):
            cols = pl.ds(pl.multiple_of(t * 256, 256), 256)
            total[:, cols] = lax.dot_general(dq_ref[...], w_vm[cols, :1536], (((1,), (1,)), ((), ())),
                                             preferred_element_type=jnp.float32)

    far(0, 0)
    far(4, 1)
    near(0, 0)
    near(4, 1)
    weight.wait()
    query_part(0, 12)
    gathered(0, 0)
    net.send("h+", mine.at[3, :128], relay.at[0], up)
    net.send("h-", mine.at[3, 128:], relay.at[1], down)
    net.recv("h+")
    net.send("r+", relay.at[0], crossed.at[:128], up)
    net.recv("h-")
    net.send("r-", relay.at[1], crossed.at[128:], down)
    gathered(4, 1)
    net.recv("r+")
    net.recv("r-")
    add(mine.at[7], crossed)

    @pl.loop(0, 12)
    def _(t):
        cols = pl.ds(pl.multiple_of(t * 256, 256), 256)
        total[:, cols] += lax.dot_general(mine[7], w_vm[cols, 1536:], (((1,), (1,)), ((), ())),
                                          preferred_element_type=jnp.float32)

    @pl.loop(0, 8)
    def _(t):
        rows = pl.ds(pl.multiple_of(t * 32, 32), 32)
        x = tok_ref[rows, :].astype(jnp.float32)
        inv_rms = lax.rsqrt(jnp.mean(x * x, axis=1, keepdims=True) + epsilon)
        scaled = total[rows, :] * gain_ref[...]
        shift = inv_rms * inv_rms * inv_rms * jnp.mean(scaled * x, axis=1, keepdims=True)
        out_ref[rows, :] = (inv_rms * scaled - x * shift).astype(jnp.bfloat16)
    net.drain()


def input_grads(tokens, gain, dq, terms, weight):
    vm, anywhere = pl.BlockSpec(memory_space=pltpu.VMEM), pl.BlockSpec(memory_space=pl.ANY)
    half = jnp.bfloat16
    return pl.pallas_call(
        grads_kernel,
        out_shape=jax.ShapeDtypeStruct((256, 3072), half),
        in_specs=[vm, vm, vm, anywhere, anywhere],
        out_specs=vm,
        scratch_shapes=[pltpu.VMEM((3072, 2560), half), pltpu.VMEM((8, 256, 1024), half),
                        pltpu.VMEM((8, 256, 1024), half), pltpu.VMEM((2, 128, 1024), half),
                        pltpu.VMEM((2, 128, 1024), half), pltpu.VMEM((2, 256, 1024), half),
                        pltpu.VMEM((2, 256, 1024), half), pltpu.VMEM((2, 128, 1024), half),
                        pltpu.VMEM((256, 1024), half), pltpu.VMEM((256, 3072), jnp.float32),
                        pltpu.SemaphoreType.DMA((24,)), pltpu.SemaphoreType.DMA((24,)),
                        pltpu.SemaphoreType.DMA((9,))],
        compiler_params=pltpu.CompilerParams(vmem_limit_bytes=60 << 20, collective_id=1, has_side_effects=True),
        name="input_grads",
    )(tokens, gain, dq, terms, weight)


def body(tokens, norm_gain, qkv_weight, block_mask, out_grad):
    gain = norm_gain[None]
    queries, pairs_all, panels = project(tokens[0], gain, qkv_weight)
    attended, query_grad, block_terms = attention(block_mask, queries, out_grad[0], pairs_all)
    token_grad = input_grads(tokens[0], gain, query_grad, block_terms, panels)
    return (attended[None], token_grad[None])


def solution(mesh):
    in_specs = (P("fsdp", "ctx", None), P(), P("fsdp", None), P(), P("fsdp", "ctx", None))
    out_specs = (P("fsdp", "ctx", None), P("fsdp", "ctx", None))
    return jax.shard_map(body, mesh=mesh, in_specs=in_specs, out_specs=out_specs, check_vma=False)
```

```python
import math

import jax
import jax.numpy as jnp
from jax import lax
from jax.experimental import pallas as pl
from jax.experimental.pallas import tpu as pltpu
from jax.sharding import PartitionSpec as P

HEADS = 12
KV_HEADS = 4
HEAD_DIM = 128
BLOCK = 128


epsilon = 1e-05
very_low = -1e30


MESH = pl.DeviceIdType.MESH
D = 3072
KEYS = pl.ds(1536, 1024)
QUERIES = pl.ds(0, 1536)


class Place:
    def __init__(self):
        self.i = lax.axis_index("ctx")
        self.f = lax.axis_index("fsdp")
        self.c = self.i % 2
        self.y = (self.i // 2) % 4
        self.z = (self.i // 8) * 2 + self.f // 4
        self.x = self.f % 4

    def ids(self, dx=0, dy=0, dz=0, swap=False):
        x, y, z = (self.x + dx) % 4, (self.y + dy) % 4, (self.z + dz) % 4
        c = 1 - self.c if swap else self.c
        return ((z // 2) * 4 + y) * 2 + c, (z % 2) * 4 + x

    def mate(self, d):
        return (self.i + d) % 16, self.f


class Net:
    def __init__(self, send_sem, recv_sem):
        self.send_sem, self.recv_sem, self.copies = send_sem, recv_sem, {}

    def send(self, name, src, dst, to):
        k = len(self.copies)
        copy = pltpu.make_async_remote_copy(
            src_ref=src, dst_ref=dst, send_sem=self.send_sem.at[k], recv_sem=self.recv_sem.at[k],
            device_id=to, device_id_type=MESH)
        copy.start()
        self.copies[name] = copy

    def recv(self, name):
        self.copies[name].wait_recv()

    def drain(self):
        for copy in self.copies.values():
            copy.wait_send()


def greet(place):
    barrier = pltpu.get_barrier_semaphore()
    peers = [place.ids(dx=1), place.ids(dx=-1), place.ids(dz=1), place.ids(dz=-1)]
    peers += [place.mate(d) for d in range(1, 16)]
    for peer in peers:
        pl.semaphore_signal(barrier, inc=1, device_id=peer, device_id_type=MESH)
    pl.semaphore_wait(barrier, len(peers))


def chosen(mask_ref, place, r):
    ones = jnp.sum(mask_ref[pl.ds(place.i * 2 + r, 1), :].astype(jnp.float32), axis=1, keepdims=True)
    return jnp.where(ones > 31.5, 1.0, 0.0)


def cut(rows, mask_ref, place, pieces):
    flags = [chosen(mask_ref, place, r) for r in range(2)]
    for j in range(16):
        cols = slice((j // 4) * 384, (j // 4 + 1) * 384)
        part = [rows[r * 128 + (j % 4) * 32:r * 128 + (j % 4 + 1) * 32, cols].astype(jnp.float32) * flags[r]
                for r in range(2)]
        pieces[j] = (part[0] + part[1]).astype(jnp.bfloat16)


def rows_at(start, count):
    return pl.ds(pl.multiple_of(start, 32), count)


class WeightGather:
    def __init__(self, net, place, tag, shard, whole, cols):
        self.net, self.p, self.tag, self.shard, self.whole, self.cols = net, place, tag, shard, whole, cols

    def at(self, dx, lo, count):
        shard_id = (self.p.f // 4) * 4 + (self.p.x + dx) % 4
        return self.whole.at[rows_at(shard_id * 384 + self.p.c * 192 + lo, count), self.cols]

    def own(self, lo, count):
        return self.shard.at[rows_at(self.p.c * 192 + lo, count), self.cols]

    def cross(self, dx, lo):
        shard_id = (1 - self.p.f // 4) * 4 + (self.p.x + dx) % 4
        return self.whole.at[rows_at(shard_id * 384 + self.p.c * 192 + lo, 96), self.cols]

    def put(self, name, piece, to, src=None):
        self.net.send(self.tag + name, piece if src is None else src, piece, to)

    def start_x(self):
        self.put("x+", self.at(0, 0, 192), self.p.ids(dx=1), self.own(0, 192))
        self.put("x-", self.at(0, 0, 192), self.p.ids(dx=-1), self.own(0, 192))

    def start_z(self):
        self.put("z+0", self.at(0, 0, 96), self.p.ids(dz=1), self.own(0, 96))
        self.put("z-0", self.at(0, 96, 96), self.p.ids(dz=-1), self.own(96, 96))

    def got(self, name):
        self.net.recv(self.tag + name)

    def first(self):
        self.got("x+")
        self.put("x+2", self.at(-1, 0, 96), self.p.ids(dx=1))
        self.got("x-")
        self.put("x-2", self.at(1, 96, 96), self.p.ids(dx=-1))
        for dx in (-1, 1):
            self.put("z+%d" % dx, self.at(dx, 0, 96), self.p.ids(dz=1))
            self.put("z-%d" % dx, self.at(dx, 96, 96), self.p.ids(dz=-1))
            self.put("c%d" % dx, self.at(dx, 0, 192), self.p.ids(swap=True))

    def second(self):
        for sign, lo, dz in (("+", 0, 1), ("-", 96, -1)):
            self.got("x%s2" % sign)
            self.put("z%s2" % sign, self.at(2, lo, 96), self.p.ids(dz=dz))
            self.put("c2%s" % sign, self.at(2, lo, 96), self.p.ids(swap=True))

    def third(self):
        for dx in (0, -1, 1, 2):
            for sign, lo in (("+", 0), ("-", 96)):
                self.got("z%s%d" % (sign, dx))
                self.put("cz%s%d" % (sign, dx), self.cross(dx, lo), self.p.ids(swap=True))

    def last(self):
        for name in ("c-1", "c1", "c2+", "c2-"):
            self.got(name)
        for dx in (0, -1, 1, 2):
            for sign in "+-":
                self.got("cz%s%d" % (sign, dx))


def project_kernel(tok_ref, gain_ref, mask_ref, do_ref, shard, q_ref, kv_all, w_all, wide_ref, w_vm, normed, kv_own,
                   relay, q_cut, do_cut, q_box, do_box, send_sem, recv_sem, local_sem):
    p = Place()
    net = Net(send_sem, recv_sem)
    greet(p)
    keys = WeightGather(net, p, "k", shard, w_vm, KEYS)
    queries = WeightGather(net, p, "q", shard, w_vm, QUERIES)
    keys.start_x()
    keys.start_z()
    mine = pltpu.make_async_copy(shard, w_vm.at[rows_at(p.f * 384, 384)], local_sem.at[0])
    mine.start()

    @pl.loop(0, 8)
    def _(t):
        rows = pl.ds(pl.multiple_of(t * 32, 32), 32)
        x = tok_ref[rows, :].astype(jnp.float32)
        inv_rms = lax.rsqrt(jnp.mean(x * x, axis=1, keepdims=True) + epsilon)
        normed[rows, :] = (x * inv_rms * gain_ref[...]).astype(jnp.bfloat16)

    cut(do_ref, mask_ref, p, do_cut)
    keys.first()
    queries.start_x()
    keys.second()
    queries.start_z()
    keys.third()
    keys.last()
    mine.wait()

    @pl.loop(0, 4)
    def _(t):
        cols = pl.ds(pl.multiple_of(t * 256, 256), 256)
        part = jnp.dot(normed[...], w_vm[:, pl.ds(pl.multiple_of(1536 + t * 256, 256), 256)],
                       preferred_element_type=jnp.float32)
        kv_own[:, cols] = part.astype(jnp.bfloat16)

    keep_keys = pltpu.make_async_copy(w_vm.at[:, KEYS], w_all.at[:, KEYS], local_sem.at[1])
    keep_keys.start()

    def home(dy=0, dz=0, lo=0, count=256):
        who, _ = p.ids(dy=dy, dz=dz)
        return kv_all.at[rows_at(who * 256 + lo, count)]

    def put(name, piece, to, src=None):
        net.send(name, piece if src is None else src, piece, to)

    swap, up, down, north, south = p.ids(swap=True), p.ids(dz=1), p.ids(dz=-1), p.ids(dy=1), p.ids(dy=-1)
    put("y+", home(), north, kv_own)
    put("y-", home(), south, kv_own)
    put("h+", relay.at[0], up, kv_own.at[:128])
    put("h-", relay.at[1], down, kv_own.at[128:])
    put("cy0", home(), swap, kv_own)
    stay = pltpu.make_async_copy(kv_own, home(), local_sem.at[2])
    stay.start()

    queries.first()
    net.recv("h+")
    put("r+", home(dz=-1, count=128), up, relay.at[0])
    net.recv("h-")
    put("r-", home(dz=1, lo=128, count=128), down, relay.at[1])
    queries.second()
    for sign, lo in (("+", 0), ("-", 128)):
        net.recv("r" + sign)
        piece = home(dz=2, lo=lo, count=128)
        put("ty+" + sign, piece, north)
        put("ty-" + sign, piece, south)
        put("ct" + sign, piece, swap)
    net.recv("y+")
    put("y+2", home(dy=-1, count=128), north)
    put("cy-", home(dy=-1), swap)
    net.recv("y-")
    put("y-2", home(dy=1, lo=128, count=128), south)
    put("cy+", home(dy=1), swap)
    queries.third()
    for d in range(1, 16):
        put("do%d" % d, do_box.at[d - 1], p.mate(d), do_cut.at[(p.i + d) % 16])
    queries.last()

    keep_queries = pltpu.make_async_copy(w_vm.at[:, QUERIES], w_all.at[:, QUERIES], local_sem.at[3])
    keep_queries.start()

    net.recv("ty++")
    put("ty+2", home(dy=-1, dz=2, count=128), north)
    put("ct-a", home(dy=-1, dz=2, count=128), swap)
    net.recv("ty--")
    put("ty-2", home(dy=1, dz=2, lo=128, count=128), south)
    put("ct+b", home(dy=1, dz=2, lo=128, count=128), swap)
    net.recv("ty+-")
    put("ct-b", home(dy=-1, dz=2, lo=128, count=128), swap)
    net.recv("ty-+")
    put("ct+a", home(dy=1, dz=2, count=128), swap)

    @pl.loop(0, 6)
    def _(t):
        cols = pl.ds(pl.multiple_of(t * 256, 256), 256)
        q_ref[:, cols] = jnp.dot(normed[...], w_vm[:, cols], preferred_element_type=jnp.float32).astype(jnp.bfloat16)

    cut(q_ref, mask_ref, p, q_cut)
    for d in range(1, 16):
        put("qq%d" % d, q_box.at[d - 1], p.mate(d), q_cut.at[(p.i + d) % 16])

    net.recv("y+2")
    put("cy2a", home(dy=2, count=128), swap)
    net.recv("y-2")
    put("cy2b", home(dy=2, lo=128, count=128), swap)
    net.recv("ty+2")
    put("ct2a", home(dy=2, dz=2, count=128), swap)
    net.recv("ty-2")
    put("ct2b", home(dy=2, dz=2, lo=128, count=128), swap)
    for name in ("cy0", "cy-", "cy+", "cy2a", "cy2b", "ct+", "ct-", "ct-a", "ct+b", "ct-b", "ct+a", "ct2a", "ct2b"):
        net.recv(name)
    for name, box, own, cols in (("qq", q_box, q_cut, slice(0, 384)), ("do", do_box, do_cut, slice(384, 768))):
        value = own[p.i]
        for d in range(1, 16):
            net.recv("%s%d" % (name, d))
            value = value + box[d - 1]
        wide_ref[:, cols] = value
    net.drain()
    for copy in (stay, keep_keys, keep_queries):
        copy.wait()


def project(tokens, gain, mask, out_grad, shard):
    vm, anywhere = pl.BlockSpec(memory_space=pltpu.VMEM), pl.BlockSpec(memory_space=pl.ANY)
    half = jnp.bfloat16
    return pl.pallas_call(
        project_kernel,
        out_shape=(jax.ShapeDtypeStruct((256, 1536), half), jax.ShapeDtypeStruct((4096, 1024), half),
                   jax.ShapeDtypeStruct((3072, 2560), half), jax.ShapeDtypeStruct((32, 768), half)),
        in_specs=[vm, vm, vm, vm, anywhere],
        out_specs=(vm, anywhere, anywhere, vm),
        scratch_shapes=[pltpu.VMEM((3072, 2560), half), pltpu.VMEM((256, 3072), half), pltpu.VMEM((256, 1024), half),
                        pltpu.VMEM((2, 128, 1024), half), pltpu.VMEM((16, 32, 384), half),
                        pltpu.VMEM((16, 32, 384), half), pltpu.VMEM((15, 32, 384), half),
                        pltpu.VMEM((15, 32, 384), half), pltpu.SemaphoreType.DMA((120,)),
                        pltpu.SemaphoreType.DMA((120,)), pltpu.SemaphoreType.DMA((4,))],
        compiler_params=pltpu.CompilerParams(vmem_limit_bytes=60 << 20, collective_id=0, has_side_effects=True),
        name="project",
    )(tokens, gain, mask, out_grad, shard)


WIDEST = 6
FACTOR = math.log2(math.e) / math.sqrt(128)
SCALE = 1.0 / math.sqrt(128)
CHUNK = 1024


def dot_nt(a, b):
    return lax.dot_general(a, b, (((1,), (1,)), ((), ())), preferred_element_type=jnp.float32)


def dot_tn(a, b):
    return lax.dot_general(a, b, (((0,), (0,)), ((), ())), preferred_element_type=jnp.float32)


def dot_nn(a, b):
    return jnp.dot(a, b, preferred_element_type=jnp.float32)


def wide_row(wide_ref, kv_ref, att_ref, dkv_ref, s_ref, head):
    kcol = pl.ds(pl.multiple_of(head * 128, 128), 128)
    vcol = pl.ds(pl.multiple_of(512 + head * 128, 128), 128)
    blank = jnp.zeros((32, 128), jnp.bfloat16)
    q = jnp.concatenate([wide_ref[:, i * 128:(i + 1) * 128] for i in range(3)] + [blank], axis=0)
    do = jnp.concatenate([wide_ref[:, 384 + i * 128:384 + (i + 1) * 128] for i in range(3)] + [blank], axis=0)
    steps = 4096 // CHUNK

    def at(c):
        return pl.ds(pl.multiple_of(c * CHUNK, CHUNK), CHUNK)

    def score(c, m):
        s = dot_nt(kv_ref[at(c), kcol], q) * FACTOR
        s_ref[at(c), :] = s
        return jnp.maximum(m, jnp.max(s, axis=0, keepdims=True))
    m = lax.fori_loop(0, steps, score, jnp.full((1, 128), -1e30, jnp.float32))

    def weigh(c, carry):
        total, acc = carry
        e = jnp.exp2(s_ref[at(c), :] - m)
        s_ref[at(c), :] = e
        total = total + jnp.sum(e, axis=0, keepdims=True)
        return total, acc + dot_tn(kv_ref[at(c), vcol], e.astype(jnp.bfloat16))
    total, acc = lax.fori_loop(0, steps, weigh,
                               (jnp.zeros((1, 128), jnp.float32), jnp.zeros((128, 128), jnp.float32)))
    inverse = 1.0 / total
    out_t = acc * inverse
    out = out_t.T.astype(jnp.bfloat16)
    for i in range(3):
        att_ref[:, i * 128:(i + 1) * 128] = out[i * 32:(i + 1) * 32]
    delta = jnp.sum(out_t.astype(jnp.bfloat16).astype(jnp.float32) * do.astype(jnp.float32).T, axis=0, keepdims=True)
    share = jnp.broadcast_to(inverse, (128, 128)).T
    do_share = (do.astype(jnp.float32) * share).astype(jnp.bfloat16)
    q_share = (q.astype(jnp.float32) * (share * SCALE)).astype(jnp.bfloat16)

    def back(c, dq_t):
        e = s_ref[at(c), :]
        ds = (e * (dot_nt(kv_ref[at(c), vcol], do) - delta)).astype(jnp.bfloat16)
        dkv_ref[at(c), vcol] = dot_nn(e.astype(jnp.bfloat16), do_share).astype(jnp.bfloat16)
        dkv_ref[at(c), kcol] = dot_nn(ds, q_share).astype(jnp.bfloat16)
        return dq_t + dot_tn(kv_ref[at(c), kcol], ds)
    dq_t = lax.fori_loop(0, steps, back, jnp.zeros((128, 128), jnp.float32))
    dq = (dq_t * (inverse * SCALE)).T.astype(jnp.bfloat16)
    for i in range(3):
        att_ref[:, 384 + i * 128:384 + (i + 1) * 128] = dq[i * 32:(i + 1) * 32]


def attention_kernel(mask_ref, q_ref, do_ref, wide_ref, kv_ref, att_ref, dq_ref, dkv_ref, wide_out, s_ref, list_ref,
                     count_ref):
    position = lax.axis_index("ctx")
    dkv_ref[...] = jnp.zeros_like(dkv_ref)
    for r in range(2):
        for b in range(WIDEST):
            list_ref[r, b] = 0

        def note(j, n):
            list_ref[r, n] = j
            return n + mask_ref[position * 2 + r, j]
        count_ref[r] = lax.fori_loop(0, 32, note, 0)

    wide_row(wide_ref, kv_ref, wide_out, dkv_ref, s_ref, position // 4)

    def unit(r, h):
        n = count_ref[r]
        rows = pl.ds(pl.multiple_of(r * 128, 128), 128)
        cols = [pl.ds(pl.multiple_of(h * 384 + i * 128, 128), 128) for i in range(3)]
        kcol = pl.ds(pl.multiple_of(h * 128, 128), 128)
        vcol = pl.ds(pl.multiple_of(512 + h * 128, 128), 128)
        q = jnp.concatenate([q_ref[rows, c] for c in cols], axis=0)
        do = jnp.concatenate([do_ref[rows, c] for c in cols], axis=0)
        places = [pl.ds(pl.multiple_of(list_ref[r, b] * 128, 128), 128) for b in range(WIDEST)]
        k = jnp.concatenate([kv_ref[w, kcol] for w in places], axis=0)
        v = jnp.concatenate([kv_ref[w, vcol] for w in places], axis=0)
        s = dot_nt(k, q) * FACTOR
        s = jnp.concatenate([s[:256]] + [jnp.where(b < n, s[b * 128:(b + 1) * 128], -1e30)
                                         for b in range(2, WIDEST)], axis=0)
        dprob = dot_nt(v, do)
        e = jnp.exp2(s - jnp.max(s, axis=0, keepdims=True))
        half = e.astype(jnp.bfloat16)
        inverse = 1.0 / jnp.sum(e, axis=0, keepdims=True)
        out_t = dot_tn(v, half) * inverse
        out = out_t.T.astype(jnp.bfloat16)
        for i in range(3):
            att_ref[rows, cols[i]] = out[i * 128:(i + 1) * 128]
        delta = jnp.sum(out_t.astype(jnp.bfloat16).astype(jnp.float32) * do.astype(jnp.float32).T, axis=0,
                        keepdims=True)
        share = jnp.broadcast_to(inverse, (128, 384)).T
        do_share = (do.astype(jnp.float32) * share).astype(jnp.bfloat16)
        q_share = (q.astype(jnp.float32) * (share * SCALE)).astype(jnp.bfloat16)
        ds = (e * (dprob - delta)).astype(jnp.bfloat16)
        dv = dot_nn(half, do_share)
        dk = dot_nn(ds, q_share)
        dq = (dot_tn(k, ds) * (inverse * SCALE)).T.astype(jnp.bfloat16)
        for i in range(3):
            dq_ref[rows, cols[i]] = dq[i * 128:(i + 1) * 128]
        for b, w in enumerate(places):
            piece = slice(b * 128, (b + 1) * 128)
            dkv_ref[w, kcol] = (dkv_ref[w, kcol].astype(jnp.float32) + dk[piece]).astype(jnp.bfloat16)
            dkv_ref[w, vcol] = (dkv_ref[w, vcol].astype(jnp.float32) + dv[piece]).astype(jnp.bfloat16)

    @pl.loop(0, 2)
    def _(r):
        @pl.when(count_ref[r] <= WIDEST)
        def _():
            @pl.loop(0, 4)
            def _(h):
                unit(r, h)

        @pl.when(count_ref[r] > WIDEST)
        def _():
            rows = pl.ds(pl.multiple_of(r * 128, 128), 128)
            att_ref[rows, :] = jnp.zeros((128, 1536), jnp.bfloat16)
            dq_ref[rows, :] = jnp.zeros((128, 1536), jnp.bfloat16)


def attention(block_mask, q, do, wide, kv):
    vm = pl.BlockSpec(memory_space=pltpu.VMEM)
    half = jnp.bfloat16
    return pl.pallas_call(
        attention_kernel,
        out_shape=(jax.ShapeDtypeStruct((256, 1536), half), jax.ShapeDtypeStruct((256, 1536), half),
                   jax.ShapeDtypeStruct((4096, 1024), half), jax.ShapeDtypeStruct((32, 768), half)),
        in_specs=[pl.BlockSpec(memory_space=pltpu.SMEM), vm, vm, vm, vm],
        out_specs=(vm, vm, vm, vm),
        scratch_shapes=[pltpu.VMEM((4096, 128), jnp.float32), pltpu.SMEM((2, 33), jnp.int32),
                        pltpu.SMEM((2,), jnp.int32)],
        compiler_params=pltpu.CompilerParams(vmem_limit_bytes=60 << 20),
        name="attention",
    )(block_mask, q, do, wide, kv)


def grads_kernel(tok_ref, gain_ref, mask_ref, part_dq, part_att, wide_ref, terms, w_all, out_ref, att_ref, w_vm, mine,
                 part, ahead, behind, after, before, relay, crossed, total, dq_ref, wide_box, send_sem, recv_sem,
                 local_sem):
    p = Place()
    net = Net(send_sem, recv_sem)
    greet(p)
    order = [(dz, dy) for dz in (2, 0) for dy in (2, 1, 3, 0)]
    swap, up, down, north, south = p.ids(swap=True), p.ids(dz=1), p.ids(dz=-1), p.ids(dy=1), p.ids(dy=-1)
    loads = {}
    for d in range(1, 16):
        net.send("w%d" % d, wide_ref, wide_box.at[p.i], p.mate(d))
    for slot, (dz, dy) in enumerate(order):
        who, _ = p.ids(dy=dy, dz=dz)
        other, _ = p.ids(dy=dy, dz=dz, swap=True)
        net.send("c%d" % slot, terms.at[rows_at(other * 256, 256)], part.at[slot], swap)
        loads[slot] = pltpu.make_async_copy(terms.at[rows_at(who * 256, 256)], mine.at[slot], local_sem.at[slot])
        loads[slot].start()
    weight = pltpu.make_async_copy(w_all, w_vm, local_sem.at[8])
    weight.start()

    def add(dst, *srcs):
        @pl.loop(0, dst.shape[0] // 64)
        def _(t):
            rows = pl.ds(pl.multiple_of(t * 64, 64), 64)
            value = dst[rows, :]
            for src in srcs:
                value = value + src[rows, :]
            dst[rows, :] = value

    def pair(slot):
        loads[slot].wait()
        net.recv("c%d" % slot)
        add(mine.at[slot], part.at[slot])

    def far(base, plane):
        pair(base)
        net.send("a%d" % plane, mine.at[base, :128], ahead.at[plane], north)
        net.send("b%d" % plane, mine.at[base, 128:], behind.at[plane], south)
        pair(base + 1)
        pair(base + 2)

    def near(base, plane):
        net.recv("a%d" % plane)
        add(mine.at[base + 1, :128], ahead.at[plane])
        net.send("f%d" % plane, mine.at[base + 1], after.at[plane], north)
        net.recv("b%d" % plane)
        add(mine.at[base + 2, 128:], behind.at[plane])
        net.send("g%d" % plane, mine.at[base + 2], before.at[plane], south)
        pair(base + 3)

    def gathered(base, plane):
        net.recv("f%d" % plane)
        net.recv("g%d" % plane)
        add(mine.at[base + 3], after.at[plane], before.at[plane])

    def join():
        wide_box[p.i] = wide_ref[...]
        for d in range(1, 16):
            net.recv("w%d" % d)
        flags = [chosen(mask_ref, p, r) for r in range(2)]
        for j in range(16):
            cols = slice((j // 4) * 384, (j // 4 + 1) * 384)
            for r in range(2):
                rows = slice(r * 128 + (j % 4) * 32, r * 128 + (j % 4 + 1) * 32)
                for out, local, lo in ((att_ref, part_att, 0), (dq_ref, part_dq, 384)):
                    value = wide_box[j, :, lo:lo + 384].astype(jnp.float32) * flags[r]
                    out[rows, cols] = (local[rows, cols].astype(jnp.float32) + value).astype(jnp.bfloat16)

    def query_part(first, last):
        @pl.loop(first, last)
        def _(t):
            cols = pl.ds(pl.multiple_of(t * 256, 256), 256)
            total[:, cols] = lax.dot_general(dq_ref[...], w_vm[cols, :1536], (((1,), (1,)), ((), ())),
                                             preferred_element_type=jnp.float32)

    far(0, 0)
    far(4, 1)
    near(0, 0)
    near(4, 1)
    join()
    weight.wait()
    query_part(0, 12)
    gathered(0, 0)
    net.send("h+", mine.at[3, :128], relay.at[0], up)
    net.send("h-", mine.at[3, 128:], relay.at[1], down)
    net.recv("h+")
    net.send("r+", relay.at[0], crossed.at[:128], up)
    net.recv("h-")
    net.send("r-", relay.at[1], crossed.at[128:], down)
    gathered(4, 1)
    net.recv("r+")
    net.recv("r-")
    add(mine.at[7], crossed)

    @pl.loop(0, 12)
    def _(t):
        cols = pl.ds(pl.multiple_of(t * 256, 256), 256)
        total[:, cols] += lax.dot_general(mine[7], w_vm[cols, 1536:], (((1,), (1,)), ((), ())),
                                          preferred_element_type=jnp.float32)

    @pl.loop(0, 8)
    def _(t):
        rows = pl.ds(pl.multiple_of(t * 32, 32), 32)
        x = tok_ref[rows, :].astype(jnp.float32)
        inv_rms = lax.rsqrt(jnp.mean(x * x, axis=1, keepdims=True) + epsilon)
        scaled = total[rows, :] * gain_ref[...]
        shift = inv_rms * inv_rms * inv_rms * jnp.mean(scaled * x, axis=1, keepdims=True)
        out_ref[rows, :] = (inv_rms * scaled - x * shift).astype(jnp.bfloat16)
    net.drain()


def input_grads(tokens, gain, mask, dq, att, wide, terms, weight):
    vm, anywhere = pl.BlockSpec(memory_space=pltpu.VMEM), pl.BlockSpec(memory_space=pl.ANY)
    half = jnp.bfloat16
    return pl.pallas_call(
        grads_kernel,
        out_shape=(jax.ShapeDtypeStruct((256, 3072), half), jax.ShapeDtypeStruct((256, 1536), half)),
        in_specs=[vm, vm, vm, vm, vm, vm, anywhere, anywhere],
        out_specs=(vm, vm),
        scratch_shapes=[pltpu.VMEM((3072, 2560), half), pltpu.VMEM((8, 256, 1024), half),
                        pltpu.VMEM((8, 256, 1024), half), pltpu.VMEM((2, 128, 1024), half),
                        pltpu.VMEM((2, 128, 1024), half), pltpu.VMEM((2, 256, 1024), half),
                        pltpu.VMEM((2, 256, 1024), half), pltpu.VMEM((2, 128, 1024), half),
                        pltpu.VMEM((256, 1024), half), pltpu.VMEM((256, 3072), jnp.float32),
                        pltpu.VMEM((256, 1536), half), pltpu.VMEM((16, 32, 768), half),
                        pltpu.SemaphoreType.DMA((40,)), pltpu.SemaphoreType.DMA((40,)),
                        pltpu.SemaphoreType.DMA((9,))],
        compiler_params=pltpu.CompilerParams(vmem_limit_bytes=60 << 20, collective_id=1, has_side_effects=True),
        name="input_grads",
    )(tokens, gain, mask, dq, att, wide, terms, weight)


def body(tokens, norm_gain, qkv_weight, block_mask, out_grad):
    gain = norm_gain[None]
    queries, pairs_all, panels, wide = project(tokens[0], gain, block_mask, out_grad[0], qkv_weight)
    part_att, part_dq, block_terms, wide_out = attention(block_mask, queries, out_grad[0], wide, pairs_all)
    token_grad, attended = input_grads(tokens[0], gain, block_mask, part_dq, part_att, wide_out, block_terms, panels)
    return (attended[None], token_grad[None])


def solution(mesh):
    in_specs = (P("fsdp", "ctx", None), P(), P("fsdp", None), P(), P("fsdp", "ctx", None))
    out_specs = (P("fsdp", "ctx", None), P("fsdp", "ctx", None))
    return jax.shard_map(body, mesh=mesh, in_specs=in_specs, out_specs=out_specs, check_vma=False)
```

```python
import math

import jax
import jax.numpy as jnp
from jax import lax
from jax.experimental import pallas as pl
from jax.experimental.pallas import tpu as pltpu
from jax.sharding import PartitionSpec as P

HEADS = 12
KV_HEADS = 4
HEAD_DIM = 128
BLOCK = 128


epsilon = 1e-05
very_low = -1e30


MESH = pl.DeviceIdType.MESH
D = 3072
KEYS = pl.ds(1536, 512)
VALUES = pl.ds(2048, 512)
PAIRS = pl.ds(1536, 1024)
QUERIES = pl.ds(0, 1536)


class Place:
    def __init__(self):
        self.i = lax.axis_index("ctx")
        self.f = lax.axis_index("fsdp")
        self.c = self.i % 2
        self.y = (self.i // 2) % 4
        self.z = (self.i // 8) * 2 + self.f // 4
        self.x = self.f % 4

    def ids(self, dx=0, dy=0, dz=0, swap=False):
        x, y, z = (self.x + dx) % 4, (self.y + dy) % 4, (self.z + dz) % 4
        c = 1 - self.c if swap else self.c
        return ((z // 2) * 4 + y) * 2 + c, (z % 2) * 4 + x

    def mate(self, d):
        return (self.i + d) % 16, self.f


class Net:
    def __init__(self, send_sem, recv_sem):
        self.send_sem, self.recv_sem, self.copies = send_sem, recv_sem, {}

    def send(self, name, src, dst, to):
        k = len(self.copies)
        copy = pltpu.make_async_remote_copy(
            src_ref=src, dst_ref=dst, send_sem=self.send_sem.at[k], recv_sem=self.recv_sem.at[k],
            device_id=to, device_id_type=MESH)
        copy.start()
        self.copies[name] = copy

    def recv(self, name):
        self.copies[name].wait_recv()

    def drain(self):
        for copy in self.copies.values():
            copy.wait_send()


def greet(place):
    barrier = pltpu.get_barrier_semaphore()
    peers = [place.ids(dx=1), place.ids(dx=-1), place.ids(dz=1), place.ids(dz=-1)]
    peers += [place.mate(d) for d in range(1, 16)]
    for peer in peers:
        pl.semaphore_signal(barrier, inc=1, device_id=peer, device_id_type=MESH)
    pl.semaphore_wait(barrier, len(peers))


def chosen(mask_ref, place, r):
    ones = jnp.sum(mask_ref[pl.ds(place.i * 2 + r, 1), :].astype(jnp.float32), axis=1, keepdims=True)
    return jnp.where(ones > 31.5, 1.0, 0.0)


def cut(rows, mask_ref, place, pieces):
    flags = [chosen(mask_ref, place, r) for r in range(2)]
    for j in range(16):
        cols = slice((j // 4) * 384, (j // 4 + 1) * 384)
        part = [rows[r * 128 + (j % 4) * 32:r * 128 + (j % 4 + 1) * 32, cols].astype(jnp.float32) * flags[r]
                for r in range(2)]
        pieces[j] = (part[0] + part[1]).astype(jnp.bfloat16)


def rows_at(start, count):
    return pl.ds(pl.multiple_of(start, 32), count)


class WeightGather:
    def __init__(self, net, place, tag, shard, whole, cols, ring=False):
        self.net, self.p, self.tag, self.shard, self.whole, self.cols = net, place, tag, shard, whole, cols
        self.ring = ring

    def at(self, dx, lo, count):
        shard_id = (self.p.f // 4) * 4 + (self.p.x + dx) % 4
        return self.whole.at[rows_at(shard_id * 384 + self.p.c * 192 + lo, count), self.cols]

    def own(self, lo, count):
        return self.shard.at[rows_at(self.p.c * 192 + lo, count), self.cols]

    def cross(self, dx, lo, count=96):
        shard_id = (1 - self.p.f // 4) * 4 + (self.p.x + dx) % 4
        return self.whole.at[rows_at(shard_id * 384 + self.p.c * 192 + lo, count), self.cols]

    def put(self, name, piece, to, src=None):
        self.net.send(self.tag + name, piece if src is None else src, piece, to)

    def start_x(self):
        self.put("x+", self.at(0, 0, 192), self.p.ids(dx=1), self.own(0, 192))
        self.put("x-", self.at(0, 0, 192), self.p.ids(dx=-1), self.own(0, 192))

    def start_z(self):
        self.put("z+0", self.at(0, 0, 96), self.p.ids(dz=1), self.own(0, 96))
        self.put("z-0", self.at(0, 96, 96), self.p.ids(dz=-1), self.own(96, 96))

    def got(self, name):
        self.net.recv(self.tag + name)

    def first(self):
        self.got("x+")
        self.put("x+2", self.at(-1, 0, 96), self.p.ids(dx=1))
        self.got("x-")
        self.put("x-2", self.at(1, 96, 96), self.p.ids(dx=-1))
        for dx in (-1, 1):
            if not self.ring:
                self.put("z+%d" % dx, self.at(dx, 0, 96), self.p.ids(dz=1))
                self.put("z-%d" % dx, self.at(dx, 96, 96), self.p.ids(dz=-1))
            self.put("c%d" % dx, self.at(dx, 0, 192), self.p.ids(swap=True))

    def second(self):
        for sign, lo, dz in (("+", 0, 1), ("-", 96, -1)):
            self.got("x%s2" % sign)
            self.put("z%s2" % sign, self.at(2, lo, 96), self.p.ids(dz=dz))
            self.put("c2%s" % sign, self.at(2, lo, 96), self.p.ids(swap=True))

    def arrive(self, dxs):
        for dx in dxs:
            for sign, lo in (("+", 0), ("-", 96)):
                self.got("z%s%d" % (sign, dx))
                self.put("cz%s%d" % (sign, dx), self.cross(dx, lo), self.p.ids(swap=True))

    def spread(self):
        for sign in (1, -1):
            self.put("X%d" % sign, self.cross(0, 0, 192), self.p.ids(dx=sign))

    def third(self):
        if not self.ring:
            self.arrive((0, -1, 1, 2))
            return
        self.arrive((2,))
        for sign in (1, -1):
            self.got("X%d" % sign)
            self.put("cX%d" % sign, self.cross(-sign, 0, 192), self.p.ids(swap=True))

    def last(self):
        for name in ("c-1", "c1", "c2+", "c2-"):
            self.got(name)
        for dx in (0, 2) if self.ring else (0, -1, 1, 2):
            for sign in "+-":
                self.got("cz%s%d" % (sign, dx))
        if self.ring:
            self.got("cX1")
            self.got("cX-1")


class BlockGather:
    def __init__(self, net, place, tag, own, whole, relay, cols):
        self.net, self.p, self.tag, self.mine, self.whole, self.relay, self.cols = net, place, tag, own, whole, relay, cols
        p = place
        self.swap, self.up, self.down = p.ids(swap=True), p.ids(dz=1), p.ids(dz=-1)
        self.north, self.south = p.ids(dy=1), p.ids(dy=-1)
        self.swapped = []

    def home(self, dy=0, dz=0, lo=0, count=256):
        who, _ = self.p.ids(dy=dy, dz=dz)
        return self.whole.at[rows_at(who * 256 + lo, count), self.cols]

    def own(self, lo=0, count=256):
        return self.mine.at[pl.ds(lo, count), self.cols]

    def put(self, name, piece, to, src=None):
        self.net.send(self.tag + name, piece if src is None else src, piece, to)

    def give(self, piece, src=None):
        name = "c%d" % len(self.swapped)
        self.put(name, piece, self.swap, src)
        self.swapped.append(name)

    def got(self, name):
        self.net.recv(self.tag + name)

    def start(self):
        self.put("h+", self.relay.at[0, :, self.cols], self.up, self.own(0, 128))
        self.put("h-", self.relay.at[1, :, self.cols], self.down, self.own(128, 128))
        self.put("y+", self.home(), self.north, self.own())
        self.put("y-", self.home(), self.south, self.own())
        self.give(self.home(), self.own())

    def relay_on(self):
        self.got("h+")
        self.put("r+", self.home(dz=-1, count=128), self.up, self.relay.at[0, :, self.cols])
        self.got("h-")
        self.put("r-", self.home(dz=1, lo=128, count=128), self.down, self.relay.at[1, :, self.cols])

    def near(self):
        self.got("y+")
        self.put("y+2", self.home(dy=-1, count=128), self.north)
        self.give(self.home(dy=-1))
        self.got("y-")
        self.put("y-2", self.home(dy=1, lo=128, count=128), self.south)
        self.give(self.home(dy=1))

    def cross(self):
        for sign, lo in (("+", 0), ("-", 128)):
            self.got("r" + sign)
            piece = self.home(dz=2, lo=lo, count=128)
            self.put("ty+" + sign, piece, self.north)
            self.put("ty-" + sign, piece, self.south)
            self.give(piece)

    def far(self):
        self.got("ty++")
        self.put("ty+2", self.home(dy=-1, dz=2, count=128), self.north)
        self.give(self.home(dy=-1, dz=2, count=128))
        self.got("ty--")
        self.put("ty-2", self.home(dy=1, dz=2, lo=128, count=128), self.south)
        self.give(self.home(dy=1, dz=2, lo=128, count=128))
        self.got("ty+-")
        self.give(self.home(dy=-1, dz=2, lo=128, count=128))
        self.got("ty-+")
        self.give(self.home(dy=1, dz=2, count=128))

    def tail(self):
        for name, dz, lo in (("y+2", 0, 0), ("y-2", 0, 128), ("ty+2", 2, 0), ("ty-2", 2, 128)):
            self.got(name)
            self.give(self.home(dy=2, dz=dz, lo=lo, count=128))

    def last(self):
        for name in self.swapped:
            self.got(name)


def project_kernel(tok_ref, gain_ref, mask_ref, do_ref, shard, q_ref, kv_all, w_all, wide_ref, w_vm, normed, kv_own,
                   relay, q_cut, do_cut, q_box, do_box, send_sem, recv_sem, local_sem):
    p = Place()
    net = Net(send_sem, recv_sem)
    greet(p)
    keys = WeightGather(net, p, "k", shard, w_vm, KEYS)
    values = WeightGather(net, p, "v", shard, w_vm, VALUES)
    queries = WeightGather(net, p, "q", shard, w_vm, QUERIES, ring=True)
    all_keys = BlockGather(net, p, "ak", kv_own, kv_all, relay, pl.ds(0, 512))
    all_values = BlockGather(net, p, "av", kv_own, kv_all, relay, pl.ds(512, 512))
    keys.start_x()
    keys.start_z()
    mine = pltpu.make_async_copy(shard, w_vm.at[rows_at(p.f * 384, 384)], local_sem.at[0])
    mine.start()

    @pl.loop(0, 8)
    def _(t):
        rows = pl.ds(pl.multiple_of(t * 32, 32), 32)
        x = tok_ref[rows, :].astype(jnp.float32)
        inv_rms = lax.rsqrt(jnp.mean(x * x, axis=1, keepdims=True) + epsilon)
        normed[rows, :] = (x * inv_rms * gain_ref[...]).astype(jnp.bfloat16)

    def pair_part(first, last):
        @pl.loop(first, last)
        def _(t):
            cols = pl.ds(pl.multiple_of(t * 256, 256), 256)
            part = jnp.dot(normed[...], w_vm[:, pl.ds(pl.multiple_of(1536 + t * 256, 256), 256)],
                           preferred_element_type=jnp.float32)
            kv_own[:, cols] = part.astype(jnp.bfloat16)

    def exchange(name, box, pieces):
        for d in range(1, 16):
            net.send("%s%d" % (name, d), pieces.at[(p.i + d) % 16], box.at[d - 1], p.mate(d))

    cut(do_ref, mask_ref, p, do_cut)
    keys.first()
    values.start_x()
    keys.second()
    values.start_z()
    keys.third()
    values.first()
    queries.start_x()
    keys.last()
    mine.wait()
    pair_part(0, 2)
    all_keys.start()
    values.second()
    all_keys.relay_on()
    queries.start_z()
    all_keys.near()
    values.third()
    all_keys.cross()
    values.last()
    pair_part(2, 4)
    all_values.start()
    stay = pltpu.make_async_copy(kv_own, kv_all.at[rows_at(p.i * 256, 256)], local_sem.at[2])
    stay.start()
    keep_pairs = pltpu.make_async_copy(w_vm.at[:, PAIRS], w_all.at[:, PAIRS], local_sem.at[1])
    keep_pairs.start()
    queries.first()
    all_values.relay_on()
    queries.arrive((0,))
    queries.spread()
    all_keys.far()
    queries.second()
    all_values.near()
    all_values.cross()
    exchange("do", do_box, do_cut)
    all_keys.tail()
    queries.third()
    queries.last()
    keep_queries = pltpu.make_async_copy(w_vm.at[:, QUERIES], w_all.at[:, QUERIES], local_sem.at[3])
    keep_queries.start()
    all_values.far()

    @pl.loop(0, 6)
    def _(t):
        cols = pl.ds(pl.multiple_of(t * 256, 256), 256)
        q_ref[:, cols] = jnp.dot(normed[...], w_vm[:, cols], preferred_element_type=jnp.float32).astype(jnp.bfloat16)

    cut(q_ref, mask_ref, p, q_cut)
    exchange("qq", q_box, q_cut)
    all_values.tail()
    all_keys.last()
    all_values.last()
    for name, box, own, cols in (("do", do_box, do_cut, slice(384, 768)), ("qq", q_box, q_cut, slice(0, 384))):
        value = own[p.i]
        for d in range(1, 16):
            net.recv("%s%d" % (name, d))
            value = value + box[d - 1]
        wide_ref[:, cols] = value
    net.drain()
    for copy in (stay, keep_pairs, keep_queries):
        copy.wait()


def project(tokens, gain, mask, out_grad, shard):
    vm, anywhere = pl.BlockSpec(memory_space=pltpu.VMEM), pl.BlockSpec(memory_space=pl.ANY)
    half = jnp.bfloat16
    return pl.pallas_call(
        project_kernel,
        out_shape=(jax.ShapeDtypeStruct((256, 1536), half), jax.ShapeDtypeStruct((4096, 1024), half),
                   jax.ShapeDtypeStruct((3072, 2560), half), jax.ShapeDtypeStruct((32, 768), half)),
        in_specs=[vm, vm, vm, vm, anywhere],
        out_specs=(vm, anywhere, anywhere, vm),
        scratch_shapes=[pltpu.VMEM((3072, 2560), half), pltpu.VMEM((256, 3072), half), pltpu.VMEM((256, 1024), half),
                        pltpu.VMEM((2, 128, 1024), half), pltpu.VMEM((16, 32, 384), half),
                        pltpu.VMEM((16, 32, 384), half), pltpu.VMEM((15, 32, 384), half),
                        pltpu.VMEM((15, 32, 384), half), pltpu.SemaphoreType.DMA((160,)),
                        pltpu.SemaphoreType.DMA((160,)), pltpu.SemaphoreType.DMA((4,))],
        compiler_params=pltpu.CompilerParams(vmem_limit_bytes=60 << 20, collective_id=0, has_side_effects=True),
        name="project",
    )(tokens, gain, mask, out_grad, shard)


WIDEST = 6
FACTOR = math.log2(math.e) / math.sqrt(128)
SCALE = 1.0 / math.sqrt(128)
CHUNK = 1024


def dot_nt(a, b):
    return lax.dot_general(a, b, (((1,), (1,)), ((), ())), preferred_element_type=jnp.float32)


def dot_tn(a, b):
    return lax.dot_general(a, b, (((0,), (0,)), ((), ())), preferred_element_type=jnp.float32)


def dot_nn(a, b):
    return jnp.dot(a, b, preferred_element_type=jnp.float32)


def wide_row(wide_ref, kv_ref, att_ref, dkv_ref, s_ref, head):
    kcol = pl.ds(pl.multiple_of(head * 128, 128), 128)
    vcol = pl.ds(pl.multiple_of(512 + head * 128, 128), 128)
    blank = jnp.zeros((32, 128), jnp.bfloat16)
    q = jnp.concatenate([wide_ref[:, i * 128:(i + 1) * 128] for i in range(3)] + [blank], axis=0)
    do = jnp.concatenate([wide_ref[:, 384 + i * 128:384 + (i + 1) * 128] for i in range(3)] + [blank], axis=0)
    steps = 4096 // CHUNK

    def at(c):
        return pl.ds(pl.multiple_of(c * CHUNK, CHUNK), CHUNK)

    def score(c, m):
        s = dot_nt(kv_ref[at(c), kcol], q) * FACTOR
        s_ref[at(c), :] = s
        return jnp.maximum(m, jnp.max(s, axis=0, keepdims=True))
    m = lax.fori_loop(0, steps, score, jnp.full((1, 128), -1e30, jnp.float32))

    def weigh(c, carry):
        total, acc = carry
        e = jnp.exp2(s_ref[at(c), :] - m)
        s_ref[at(c), :] = e
        total = total + jnp.sum(e, axis=0, keepdims=True)
        return total, acc + dot_tn(kv_ref[at(c), vcol], e.astype(jnp.bfloat16))
    total, acc = lax.fori_loop(0, steps, weigh,
                               (jnp.zeros((1, 128), jnp.float32), jnp.zeros((128, 128), jnp.float32)))
    inverse = 1.0 / total
    out_t = acc * inverse
    out = out_t.T.astype(jnp.bfloat16)
    for i in range(3):
        att_ref[:, i * 128:(i + 1) * 128] = out[i * 32:(i + 1) * 32]
    delta = jnp.sum(out_t.astype(jnp.bfloat16).astype(jnp.float32) * do.astype(jnp.float32).T, axis=0, keepdims=True)
    share = jnp.broadcast_to(inverse, (128, 128)).T
    do_share = (do.astype(jnp.float32) * share).astype(jnp.bfloat16)
    q_share = (q.astype(jnp.float32) * (share * SCALE)).astype(jnp.bfloat16)

    def back(c, dq_t):
        e = s_ref[at(c), :]
        ds = (e * (dot_nt(kv_ref[at(c), vcol], do) - delta)).astype(jnp.bfloat16)
        dkv_ref[at(c), vcol] = dot_nn(e.astype(jnp.bfloat16), do_share).astype(jnp.bfloat16)
        dkv_ref[at(c), kcol] = dot_nn(ds, q_share).astype(jnp.bfloat16)
        return dq_t + dot_tn(kv_ref[at(c), kcol], ds)
    dq_t = lax.fori_loop(0, steps, back, jnp.zeros((128, 128), jnp.float32))
    dq = (dq_t * (inverse * SCALE)).T.astype(jnp.bfloat16)
    for i in range(3):
        att_ref[:, 384 + i * 128:384 + (i + 1) * 128] = dq[i * 32:(i + 1) * 32]


def attention_kernel(mask_ref, q_ref, do_ref, wide_ref, kv_ref, att_ref, dq_ref, dkv_ref, wide_out, s_ref, list_ref,
                     count_ref):
    position = lax.axis_index("ctx")
    dkv_ref[...] = jnp.zeros_like(dkv_ref)
    for r in range(2):
        for b in range(WIDEST):
            list_ref[r, b] = 0

        def note(j, n):
            list_ref[r, n] = j
            return n + mask_ref[position * 2 + r, j]
        count_ref[r] = lax.fori_loop(0, 32, note, 0)

    wide_row(wide_ref, kv_ref, wide_out, dkv_ref, s_ref, position // 4)

    def unit(r, h):
        n = count_ref[r]
        rows = pl.ds(pl.multiple_of(r * 128, 128), 128)
        cols = [pl.ds(pl.multiple_of(h * 384 + i * 128, 128), 128) for i in range(3)]
        kcol = pl.ds(pl.multiple_of(h * 128, 128), 128)
        vcol = pl.ds(pl.multiple_of(512 + h * 128, 128), 128)
        q = jnp.concatenate([q_ref[rows, c] for c in cols], axis=0)
        do = jnp.concatenate([do_ref[rows, c] for c in cols], axis=0)
        places = [pl.ds(pl.multiple_of(list_ref[r, b] * 128, 128), 128) for b in range(WIDEST)]
        k = jnp.concatenate([kv_ref[w, kcol] for w in places], axis=0)
        v = jnp.concatenate([kv_ref[w, vcol] for w in places], axis=0)
        s = dot_nt(k, q) * FACTOR
        s = jnp.concatenate([s[:256]] + [jnp.where(b < n, s[b * 128:(b + 1) * 128], -1e30)
                                         for b in range(2, WIDEST)], axis=0)
        dprob = dot_nt(v, do)
        e = jnp.exp2(s - jnp.max(s, axis=0, keepdims=True))
        half = e.astype(jnp.bfloat16)
        inverse = 1.0 / jnp.sum(e, axis=0, keepdims=True)
        out_t = dot_tn(v, half) * inverse
        out = out_t.T.astype(jnp.bfloat16)
        for i in range(3):
            att_ref[rows, cols[i]] = out[i * 128:(i + 1) * 128]
        delta = jnp.sum(out_t.astype(jnp.bfloat16).astype(jnp.float32) * do.astype(jnp.float32).T, axis=0,
                        keepdims=True)
        share = jnp.broadcast_to(inverse, (128, 384)).T
        do_share = (do.astype(jnp.float32) * share).astype(jnp.bfloat16)
        q_share = (q.astype(jnp.float32) * (share * SCALE)).astype(jnp.bfloat16)
        ds = (e * (dprob - delta)).astype(jnp.bfloat16)
        dv = dot_nn(half, do_share)
        dk = dot_nn(ds, q_share)
        dq = (dot_tn(k, ds) * (inverse * SCALE)).T.astype(jnp.bfloat16)
        for i in range(3):
            dq_ref[rows, cols[i]] = dq[i * 128:(i + 1) * 128]
        for b, w in enumerate(places):
            piece = slice(b * 128, (b + 1) * 128)
            dkv_ref[w, kcol] = (dkv_ref[w, kcol].astype(jnp.float32) + dk[piece]).astype(jnp.bfloat16)
            dkv_ref[w, vcol] = (dkv_ref[w, vcol].astype(jnp.float32) + dv[piece]).astype(jnp.bfloat16)

    @pl.loop(0, 2)
    def _(r):
        @pl.when(count_ref[r] <= WIDEST)
        def _():
            @pl.loop(0, 4)
            def _(h):
                unit(r, h)

        @pl.when(count_ref[r] > WIDEST)
        def _():
            rows = pl.ds(pl.multiple_of(r * 128, 128), 128)
            att_ref[rows, :] = jnp.zeros((128, 1536), jnp.bfloat16)
            dq_ref[rows, :] = jnp.zeros((128, 1536), jnp.bfloat16)


def attention(block_mask, q, do, wide, kv):
    vm = pl.BlockSpec(memory_space=pltpu.VMEM)
    half = jnp.bfloat16
    return pl.pallas_call(
        attention_kernel,
        out_shape=(jax.ShapeDtypeStruct((256, 1536), half), jax.ShapeDtypeStruct((256, 1536), half),
                   jax.ShapeDtypeStruct((4096, 1024), half), jax.ShapeDtypeStruct((32, 768), half)),
        in_specs=[pl.BlockSpec(memory_space=pltpu.SMEM), vm, vm, vm, vm],
        out_specs=(vm, vm, vm, vm),
        scratch_shapes=[pltpu.VMEM((4096, 128), jnp.float32), pltpu.SMEM((2, 33), jnp.int32),
                        pltpu.SMEM((2,), jnp.int32)],
        compiler_params=pltpu.CompilerParams(vmem_limit_bytes=60 << 20),
        name="attention",
    )(block_mask, q, do, wide, kv)


def grads_kernel(tok_ref, gain_ref, mask_ref, part_dq, part_att, wide_ref, terms, w_all, out_ref, att_ref, w_vm, mine,
                 part, ahead, behind, after, before, relay, crossed, total, dq_ref, wide_box, send_sem, recv_sem,
                 local_sem):
    p = Place()
    net = Net(send_sem, recv_sem)
    greet(p)
    order = [(dz, dy) for dz in (2, 0) for dy in (2, 1, 3, 0)]
    swap, up, down, north, south = p.ids(swap=True), p.ids(dz=1), p.ids(dz=-1), p.ids(dy=1), p.ids(dy=-1)
    loads = {}
    for d in range(1, 16):
        net.send("w%d" % d, wide_ref, wide_box.at[p.i], p.mate(d))
    for slot, (dz, dy) in enumerate(order):
        who, _ = p.ids(dy=dy, dz=dz)
        other, _ = p.ids(dy=dy, dz=dz, swap=True)
        net.send("c%d" % slot, terms.at[rows_at(other * 256, 256)], part.at[slot], swap)
        loads[slot] = pltpu.make_async_copy(terms.at[rows_at(who * 256, 256)], mine.at[slot], local_sem.at[slot])
        loads[slot].start()
    weight = pltpu.make_async_copy(w_all, w_vm, local_sem.at[8])
    weight.start()

    def add(dst, *srcs):
        @pl.loop(0, dst.shape[0] // 64)
        def _(t):
            rows = pl.ds(pl.multiple_of(t * 64, 64), 64)
            value = dst[rows, :]
            for src in srcs:
                value = value + src[rows, :]
            dst[rows, :] = value

    def pair(slot):
        loads[slot].wait()
        net.recv("c%d" % slot)
        add(mine.at[slot], part.at[slot])

    def far(base, plane):
        pair(base)
        net.send("a%d" % plane, mine.at[base, :128], ahead.at[plane], north)
        net.send("b%d" % plane, mine.at[base, 128:], behind.at[plane], south)
        pair(base + 1)
        pair(base + 2)

    def near(base, plane):
        net.recv("a%d" % plane)
        add(mine.at[base + 1, :128], ahead.at[plane])
        net.send("f%d" % plane, mine.at[base + 1], after.at[plane], north)
        net.recv("b%d" % plane)
        add(mine.at[base + 2, 128:], behind.at[plane])
        net.send("g%d" % plane, mine.at[base + 2], before.at[plane], south)
        pair(base + 3)

    def gathered(base, plane):
        net.recv("f%d" % plane)
        net.recv("g%d" % plane)
        add(mine.at[base + 3], after.at[plane], before.at[plane])

    def join():
        wide_box[p.i] = wide_ref[...]
        for d in range(1, 16):
            net.recv("w%d" % d)
        flags = [chosen(mask_ref, p, r) for r in range(2)]
        for j in range(16):
            cols = slice((j // 4) * 384, (j // 4 + 1) * 384)
            for r in range(2):
                rows = slice(r * 128 + (j % 4) * 32, r * 128 + (j % 4 + 1) * 32)
                for out, local, lo in ((att_ref, part_att, 0), (dq_ref, part_dq, 384)):
                    value = wide_box[j, :, lo:lo + 384].astype(jnp.float32) * flags[r]
                    out[rows, cols] = (local[rows, cols].astype(jnp.float32) + value).astype(jnp.bfloat16)

    def query_part(first, last):
        @pl.loop(first, last)
        def _(t):
            cols = pl.ds(pl.multiple_of(t * 256, 256), 256)
            total[:, cols] = lax.dot_general(dq_ref[...], w_vm[cols, :1536], (((1,), (1,)), ((), ())),
                                             preferred_element_type=jnp.float32)

    far(0, 0)
    far(4, 1)
    near(0, 0)
    near(4, 1)
    join()
    weight.wait()
    query_part(0, 12)
    gathered(0, 0)
    net.send("h+", mine.at[3, :128], relay.at[0], up)
    net.send("h-", mine.at[3, 128:], relay.at[1], down)
    net.recv("h+")
    net.send("r+", relay.at[0], crossed.at[:128], up)
    net.recv("h-")
    net.send("r-", relay.at[1], crossed.at[128:], down)
    gathered(4, 1)
    net.recv("r+")
    net.recv("r-")
    add(mine.at[7], crossed)

    @pl.loop(0, 12)
    def _(t):
        cols = pl.ds(pl.multiple_of(t * 256, 256), 256)
        total[:, cols] += lax.dot_general(mine[7], w_vm[cols, 1536:], (((1,), (1,)), ((), ())),
                                          preferred_element_type=jnp.float32)

    @pl.loop(0, 8)
    def _(t):
        rows = pl.ds(pl.multiple_of(t * 32, 32), 32)
        x = tok_ref[rows, :].astype(jnp.float32)
        inv_rms = lax.rsqrt(jnp.mean(x * x, axis=1, keepdims=True) + epsilon)
        scaled = total[rows, :] * gain_ref[...]
        shift = inv_rms * inv_rms * inv_rms * jnp.mean(scaled * x, axis=1, keepdims=True)
        out_ref[rows, :] = (inv_rms * scaled - x * shift).astype(jnp.bfloat16)
    net.drain()


def input_grads(tokens, gain, mask, dq, att, wide, terms, weight):
    vm, anywhere = pl.BlockSpec(memory_space=pltpu.VMEM), pl.BlockSpec(memory_space=pl.ANY)
    half = jnp.bfloat16
    return pl.pallas_call(
        grads_kernel,
        out_shape=(jax.ShapeDtypeStruct((256, 3072), half), jax.ShapeDtypeStruct((256, 1536), half)),
        in_specs=[vm, vm, vm, vm, vm, vm, anywhere, anywhere],
        out_specs=(vm, vm),
        scratch_shapes=[pltpu.VMEM((3072, 2560), half), pltpu.VMEM((8, 256, 1024), half),
                        pltpu.VMEM((8, 256, 1024), half), pltpu.VMEM((2, 128, 1024), half),
                        pltpu.VMEM((2, 128, 1024), half), pltpu.VMEM((2, 256, 1024), half),
                        pltpu.VMEM((2, 256, 1024), half), pltpu.VMEM((2, 128, 1024), half),
                        pltpu.VMEM((256, 1024), half), pltpu.VMEM((256, 3072), jnp.float32),
                        pltpu.VMEM((256, 1536), half), pltpu.VMEM((16, 32, 768), half),
                        pltpu.SemaphoreType.DMA((40,)), pltpu.SemaphoreType.DMA((40,)),
                        pltpu.SemaphoreType.DMA((9,))],
        compiler_params=pltpu.CompilerParams(vmem_limit_bytes=60 << 20, collective_id=1, has_side_effects=True),
        name="input_grads",
    )(tokens, gain, mask, dq, att, wide, terms, weight)


def body(tokens, norm_gain, qkv_weight, block_mask, out_grad):
    gain = norm_gain[None]
    queries, pairs_all, panels, wide = project(tokens[0], gain, block_mask, out_grad[0], qkv_weight)
    part_att, part_dq, block_terms, wide_out = attention(block_mask, queries, out_grad[0], wide, pairs_all)
    token_grad, attended = input_grads(tokens[0], gain, block_mask, part_dq, part_att, wide_out, block_terms, panels)
    return (attended[None], token_grad[None])


def solution(mesh):
    in_specs = (P("fsdp", "ctx", None), P(), P("fsdp", None), P(), P("fsdp", "ctx", None))
    out_specs = (P("fsdp", "ctx", None), P("fsdp", "ctx", None))
    return jax.shard_map(body, mesh=mesh, in_specs=in_specs, out_specs=out_specs, check_vma=False)
```

```python
import math

import jax
import jax.numpy as jnp
from jax import lax
from jax.experimental import pallas as pl
from jax.experimental.pallas import tpu as pltpu
from jax.sharding import PartitionSpec as P

HEADS = 12
KV_HEADS = 4
HEAD_DIM = 128
BLOCK = 128


epsilon = 1e-05
very_low = -1e30


MESH = pl.DeviceIdType.MESH
D = 3072
KEYS = pl.ds(1536, 512)
VALUES = pl.ds(2048, 512)
PAIRS = pl.ds(1536, 1024)
QUERIES = pl.ds(0, 1536)


class Place:
    def __init__(self):
        self.i = lax.axis_index("ctx")
        self.f = lax.axis_index("fsdp")
        self.c = self.i % 2
        self.y = (self.i // 2) % 4
        self.z = (self.i // 8) * 2 + self.f // 4
        self.x = self.f % 4

    def ids(self, dx=0, dy=0, dz=0, swap=False):
        x, y, z = (self.x + dx) % 4, (self.y + dy) % 4, (self.z + dz) % 4
        c = 1 - self.c if swap else self.c
        return ((z // 2) * 4 + y) * 2 + c, (z % 2) * 4 + x

    def mate(self, d):
        return (self.i + d) % 16, self.f


class Net:
    def __init__(self, send_sem, recv_sem):
        self.send_sem, self.recv_sem, self.copies = send_sem, recv_sem, {}

    def send(self, name, src, dst, to):
        k = len(self.copies)
        copy = pltpu.make_async_remote_copy(
            src_ref=src, dst_ref=dst, send_sem=self.send_sem.at[k], recv_sem=self.recv_sem.at[k],
            device_id=to, device_id_type=MESH)
        copy.start()
        self.copies[name] = copy

    def recv(self, name):
        self.copies[name].wait_recv()

    def drain(self):
        for copy in self.copies.values():
            copy.wait_send()


def greet(place):
    barrier = pltpu.get_barrier_semaphore()
    peers = [place.ids(dx=1), place.ids(dx=-1), place.ids(dz=1), place.ids(dz=-1)]
    peers += [place.mate(d) for d in range(1, 16)]
    for peer in peers:
        pl.semaphore_signal(barrier, inc=1, device_id=peer, device_id_type=MESH)
    pl.semaphore_wait(barrier, len(peers))


def chosen(mask_ref, place, r):
    ones = jnp.sum(mask_ref[pl.ds(place.i * 2 + r, 1), :].astype(jnp.float32), axis=1, keepdims=True)
    return jnp.where(ones > 31.5, 1.0, 0.0)


def cut(rows, mask_ref, place, pieces):
    flags = [chosen(mask_ref, place, r) for r in range(2)]
    for j in range(16):
        cols = slice((j // 4) * 384, (j // 4 + 1) * 384)
        part = [rows[r * 128 + (j % 4) * 32:r * 128 + (j % 4 + 1) * 32, cols].astype(jnp.float32) * flags[r]
                for r in range(2)]
        pieces[j] = (part[0] + part[1]).astype(jnp.bfloat16)


def rows_at(start, count):
    return pl.ds(pl.multiple_of(start, 32), count)


class WeightGather:
    def __init__(self, net, place, tag, shard, whole, cols, ring=False):
        self.net, self.p, self.tag, self.shard, self.whole, self.cols = net, place, tag, shard, whole, cols
        self.ring = ring

    def at(self, dx, lo, count):
        shard_id = (self.p.f // 4) * 4 + (self.p.x + dx) % 4
        return self.whole.at[rows_at(shard_id * 384 + self.p.c * 192 + lo, count), self.cols]

    def own(self, lo, count):
        return self.shard.at[rows_at(self.p.c * 192 + lo, count), self.cols]

    def cross(self, dx, lo, count=96):
        shard_id = (1 - self.p.f // 4) * 4 + (self.p.x + dx) % 4
        return self.whole.at[rows_at(shard_id * 384 + self.p.c * 192 + lo, count), self.cols]

    def put(self, name, piece, to, src=None):
        self.net.send(self.tag + name, piece if src is None else src, piece, to)

    def start_x(self):
        self.put("x+", self.at(0, 0, 192), self.p.ids(dx=1), self.own(0, 192))
        self.put("x-", self.at(0, 0, 192), self.p.ids(dx=-1), self.own(0, 192))

    def start_z(self):
        self.put("z+0", self.at(0, 0, 96), self.p.ids(dz=1), self.own(0, 96))
        self.put("z-0", self.at(0, 96, 96), self.p.ids(dz=-1), self.own(96, 96))

    def got(self, name):
        self.net.recv(self.tag + name)

    def first(self):
        self.got("x+")
        self.put("x+2", self.at(-1, 0, 96), self.p.ids(dx=1))
        self.got("x-")
        self.put("x-2", self.at(1, 96, 96), self.p.ids(dx=-1))
        for dx in (-1, 1):
            if not self.ring:
                self.put("z+%d" % dx, self.at(dx, 0, 96), self.p.ids(dz=1))
                self.put("z-%d" % dx, self.at(dx, 96, 96), self.p.ids(dz=-1))
            self.put("c%d" % dx, self.at(dx, 0, 192), self.p.ids(swap=True))

    def second(self):
        for sign, lo, dz in (("+", 0, 1), ("-", 96, -1)):
            self.got("x%s2" % sign)
            self.put("z%s2" % sign, self.at(2, lo, 96), self.p.ids(dz=dz))
            self.put("c2%s" % sign, self.at(2, lo, 96), self.p.ids(swap=True))

    def arrive(self, dxs):
        for dx in dxs:
            for sign, lo in (("+", 0), ("-", 96)):
                self.got("z%s%d" % (sign, dx))
                self.put("cz%s%d" % (sign, dx), self.cross(dx, lo), self.p.ids(swap=True))

    def spread(self):
        for sign in (1, -1):
            self.put("X%d" % sign, self.cross(0, 0, 192), self.p.ids(dx=sign))

    def third(self):
        if not self.ring:
            self.arrive((0, -1, 1, 2))
            return
        self.arrive((2,))
        for sign in (1, -1):
            self.got("X%d" % sign)
            self.put("cX%d" % sign, self.cross(-sign, 0, 192), self.p.ids(swap=True))

    def last(self):
        for name in ("c-1", "c1", "c2+", "c2-"):
            self.got(name)
        for dx in (0, 2) if self.ring else (0, -1, 1, 2):
            for sign in "+-":
                self.got("cz%s%d" % (sign, dx))
        if self.ring:
            self.got("cX1")
            self.got("cX-1")


class BlockGather:
    def __init__(self, net, place, tag, own, whole, relay, cols):
        self.net, self.p, self.tag, self.mine, self.whole, self.relay, self.cols = net, place, tag, own, whole, relay, cols
        p = place
        self.swap, self.up, self.down = p.ids(swap=True), p.ids(dz=1), p.ids(dz=-1)
        self.north, self.south = p.ids(dy=1), p.ids(dy=-1)
        self.swapped = []

    def home(self, dy=0, dz=0, lo=0, count=256):
        who, _ = self.p.ids(dy=dy, dz=dz)
        return self.whole.at[rows_at(who * 256 + lo, count), self.cols]

    def own(self, lo=0, count=256):
        return self.mine.at[pl.ds(lo, count), self.cols]

    def put(self, name, piece, to, src=None):
        self.net.send(self.tag + name, piece if src is None else src, piece, to)

    def give(self, piece, src=None):
        name = "c%d" % len(self.swapped)
        self.put(name, piece, self.swap, src)
        self.swapped.append(name)

    def got(self, name):
        self.net.recv(self.tag + name)

    def start(self):
        self.put("h+", self.relay.at[0, :, self.cols], self.up, self.own(0, 128))
        self.put("h-", self.relay.at[1, :, self.cols], self.down, self.own(128, 128))
        self.put("y+", self.home(), self.north, self.own())
        self.put("y-", self.home(), self.south, self.own())
        self.give(self.home(), self.own())

    def relay_on(self):
        self.got("h+")
        self.put("r+", self.home(dz=-1, count=128), self.up, self.relay.at[0, :, self.cols])
        self.got("h-")
        self.put("r-", self.home(dz=1, lo=128, count=128), self.down, self.relay.at[1, :, self.cols])

    def near(self):
        self.got("y+")
        self.put("y+2", self.home(dy=-1, count=128), self.north)
        self.give(self.home(dy=-1))
        self.got("y-")
        self.put("y-2", self.home(dy=1, lo=128, count=128), self.south)
        self.give(self.home(dy=1))

    def cross(self):
        for sign, lo in (("+", 0), ("-", 128)):
            self.got("r" + sign)
            piece = self.home(dz=2, lo=lo, count=128)
            self.put("ty+" + sign, piece, self.north)
            self.put("ty-" + sign, piece, self.south)
            self.give(piece)

    def far(self):
        self.got("ty++")
        self.put("ty+2", self.home(dy=-1, dz=2, count=128), self.north)
        self.give(self.home(dy=-1, dz=2, count=128))
        self.got("ty--")
        self.put("ty-2", self.home(dy=1, dz=2, lo=128, count=128), self.south)
        self.give(self.home(dy=1, dz=2, lo=128, count=128))
        self.got("ty+-")
        self.give(self.home(dy=-1, dz=2, lo=128, count=128))
        self.got("ty-+")
        self.give(self.home(dy=1, dz=2, count=128))

    def tail(self):
        for name, dz, lo in (("y+2", 0, 0), ("y-2", 0, 128), ("ty+2", 2, 0), ("ty-2", 2, 128)):
            self.got(name)
            self.give(self.home(dy=2, dz=dz, lo=lo, count=128))

    def last(self):
        for name in self.swapped:
            self.got(name)


def project_kernel(tok_ref, gain_ref, mask_ref, do_ref, shard, q_ref, kv_all, w_all, wide_ref, w_vm, normed, kv_own,
                   relay, q_cut, do_cut, q_box, do_box, send_sem, recv_sem, local_sem):
    p = Place()
    net = Net(send_sem, recv_sem)
    greet(p)
    keys = WeightGather(net, p, "k", shard, w_vm, KEYS)
    values = WeightGather(net, p, "v", shard, w_vm, VALUES)
    queries = WeightGather(net, p, "q", shard, w_vm, QUERIES, ring=True)
    all_keys = BlockGather(net, p, "ak", kv_own, kv_all, relay, pl.ds(0, 512))
    all_values = BlockGather(net, p, "av", kv_own, kv_all, relay, pl.ds(512, 512))
    keys.start_x()
    keys.start_z()
    mine = pltpu.make_async_copy(shard, w_vm.at[rows_at(p.f * 384, 384)], local_sem.at[0])
    mine.start()

    @pl.loop(0, 8)
    def _(t):
        rows = pl.ds(pl.multiple_of(t * 32, 32), 32)
        x = tok_ref[rows, :].astype(jnp.float32)
        inv_rms = lax.rsqrt(jnp.mean(x * x, axis=1, keepdims=True) + epsilon)
        normed[rows, :] = (x * inv_rms * gain_ref[...]).astype(jnp.bfloat16)

    def pair_part(first, last):
        @pl.loop(first, last)
        def _(t):
            cols = pl.ds(pl.multiple_of(t * 256, 256), 256)
            part = jnp.dot(normed[...], w_vm[:, pl.ds(pl.multiple_of(1536 + t * 256, 256), 256)],
                           preferred_element_type=jnp.float32)
            kv_own[:, cols] = part.astype(jnp.bfloat16)

    def exchange(name, box, pieces):
        for d in range(1, 16):
            net.send("%s%d" % (name, d), pieces.at[(p.i + d) % 16], box.at[d - 1], p.mate(d))

    cut(do_ref, mask_ref, p, do_cut)
    keys.first()
    values.start_x()
    keys.second()
    values.start_z()
    keys.third()
    values.first()
    queries.start_x()
    keys.last()
    mine.wait()
    pair_part(0, 2)
    all_keys.start()
    values.second()
    all_keys.relay_on()
    queries.start_z()
    all_keys.near()
    values.third()
    all_keys.cross()
    values.last()
    pair_part(2, 4)
    all_values.start()
    stay = pltpu.make_async_copy(kv_own, kv_all.at[rows_at(p.i * 256, 256)], local_sem.at[2])
    stay.start()
    keep_pairs = pltpu.make_async_copy(w_vm.at[:, PAIRS], w_all.at[:, PAIRS], local_sem.at[1])
    keep_pairs.start()
    queries.first()
    all_values.relay_on()
    queries.arrive((0,))
    queries.spread()
    all_keys.far()
    queries.second()
    all_values.near()
    all_values.cross()
    exchange("do", do_box, do_cut)
    all_keys.tail()
    queries.third()
    queries.last()
    keep_queries = pltpu.make_async_copy(w_vm.at[:, QUERIES], w_all.at[:, QUERIES], local_sem.at[3])
    keep_queries.start()
    all_values.far()

    @pl.loop(0, 6)
    def _(t):
        cols = pl.ds(pl.multiple_of(t * 256, 256), 256)
        q_ref[:, cols] = jnp.dot(normed[...], w_vm[:, cols], preferred_element_type=jnp.float32).astype(jnp.bfloat16)

    cut(q_ref, mask_ref, p, q_cut)
    exchange("qq", q_box, q_cut)
    all_values.tail()
    all_keys.last()
    all_values.last()
    for name, box, own, cols in (("do", do_box, do_cut, slice(384, 768)), ("qq", q_box, q_cut, slice(0, 384))):
        value = own[p.i]
        for d in range(1, 16):
            net.recv("%s%d" % (name, d))
            value = value + box[d - 1]
        wide_ref[:, cols] = value
    net.drain()
    for copy in (stay, keep_pairs, keep_queries):
        copy.wait()


def project(tokens, gain, mask, out_grad, shard):
    vm, anywhere = pl.BlockSpec(memory_space=pltpu.VMEM), pl.BlockSpec(memory_space=pl.ANY)
    half = jnp.bfloat16
    return pl.pallas_call(
        project_kernel,
        out_shape=(jax.ShapeDtypeStruct((256, 1536), half), jax.ShapeDtypeStruct((4096, 1024), half),
                   jax.ShapeDtypeStruct((3072, 2560), half), jax.ShapeDtypeStruct((32, 768), half)),
        in_specs=[vm, vm, vm, vm, anywhere],
        out_specs=(vm, anywhere, anywhere, vm),
        scratch_shapes=[pltpu.VMEM((3072, 2560), half), pltpu.VMEM((256, 3072), half), pltpu.VMEM((256, 1024), half),
                        pltpu.VMEM((2, 128, 1024), half), pltpu.VMEM((16, 32, 384), half),
                        pltpu.VMEM((16, 32, 384), half), pltpu.VMEM((15, 32, 384), half),
                        pltpu.VMEM((15, 32, 384), half), pltpu.SemaphoreType.DMA((160,)),
                        pltpu.SemaphoreType.DMA((160,)), pltpu.SemaphoreType.DMA((4,))],
        compiler_params=pltpu.CompilerParams(vmem_limit_bytes=60 << 20, collective_id=0, has_side_effects=True),
        name="project",
    )(tokens, gain, mask, out_grad, shard)


WIDEST = 6
FACTOR = math.log2(math.e) / math.sqrt(128)
SCALE = 1.0 / math.sqrt(128)
CHUNK = 1024


def dot_nt(a, b):
    return lax.dot_general(a, b, (((1,), (1,)), ((), ())), preferred_element_type=jnp.float32)


def dot_tn(a, b):
    return lax.dot_general(a, b, (((0,), (0,)), ((), ())), preferred_element_type=jnp.float32)


def dot_nn(a, b):
    return jnp.dot(a, b, preferred_element_type=jnp.float32)


def wide_row(wide_ref, kv_ref, att_ref, dkv_ref, s_ref, head):
    kcol = pl.ds(pl.multiple_of(head * 128, 128), 128)
    vcol = pl.ds(pl.multiple_of(512 + head * 128, 128), 128)
    blank = jnp.zeros((32, 128), jnp.bfloat16)
    q = jnp.concatenate([wide_ref[:, i * 128:(i + 1) * 128] for i in range(3)] + [blank], axis=0)
    do = jnp.concatenate([wide_ref[:, 384 + i * 128:384 + (i + 1) * 128] for i in range(3)] + [blank], axis=0)
    steps = 4096 // CHUNK

    def at(c):
        return pl.ds(pl.multiple_of(c * CHUNK, CHUNK), CHUNK)

    def score(c, m):
        s = dot_nt(kv_ref[at(c), kcol], q) * FACTOR
        s_ref[at(c), :] = s
        return jnp.maximum(m, jnp.max(s, axis=0, keepdims=True))
    m = lax.fori_loop(0, steps, score, jnp.full((1, 128), -1e30, jnp.float32))

    def weigh(c, carry):
        total, acc = carry
        e = jnp.exp2(s_ref[at(c), :] - m)
        s_ref[at(c), :] = e
        total = total + jnp.sum(e, axis=0, keepdims=True)
        return total, acc + dot_tn(kv_ref[at(c), vcol], e.astype(jnp.bfloat16))
    total, acc = lax.fori_loop(0, steps, weigh,
                               (jnp.zeros((1, 128), jnp.float32), jnp.zeros((128, 128), jnp.float32)))
    inverse = 1.0 / total
    out_t = acc * inverse
    out = out_t.T.astype(jnp.bfloat16)
    for i in range(3):
        att_ref[:, i * 128:(i + 1) * 128] = out[i * 32:(i + 1) * 32]
    delta = jnp.sum(out_t.astype(jnp.bfloat16).astype(jnp.float32) * do.astype(jnp.float32).T, axis=0, keepdims=True)
    share = jnp.broadcast_to(inverse, (128, 128)).T
    do_share = (do.astype(jnp.float32) * share).astype(jnp.bfloat16)
    q_share = (q.astype(jnp.float32) * (share * SCALE)).astype(jnp.bfloat16)

    def back(c, dq_t):
        e = s_ref[at(c), :]
        ds = (e * (dot_nt(kv_ref[at(c), vcol], do) - delta)).astype(jnp.bfloat16)
        dkv_ref[at(c), vcol] = dot_nn(e.astype(jnp.bfloat16), do_share).astype(jnp.bfloat16)
        dkv_ref[at(c), kcol] = dot_nn(ds, q_share).astype(jnp.bfloat16)
        return dq_t + dot_tn(kv_ref[at(c), kcol], ds)
    dq_t = lax.fori_loop(0, steps, back, jnp.zeros((128, 128), jnp.float32))
    dq = (dq_t * (inverse * SCALE)).T.astype(jnp.bfloat16)
    for i in range(3):
        att_ref[:, 384 + i * 128:384 + (i + 1) * 128] = dq[i * 32:(i + 1) * 32]


def attention_kernel(mask_ref, q_ref, do_ref, wide_ref, kv_ref, att_ref, dq_ref, dkv_ref, wide_out, s_ref, list_ref,
                     count_ref):
    position = lax.axis_index("ctx")
    dkv_ref[...] = jnp.zeros_like(dkv_ref)
    for r in range(2):
        for b in range(WIDEST):
            list_ref[r, b] = 0

        def note(j, n):
            list_ref[r, n] = j
            return n + mask_ref[position * 2 + r, j]
        count_ref[r] = lax.fori_loop(0, 32, note, 0)

    wide_row(wide_ref, kv_ref, wide_out, dkv_ref, s_ref, position // 4)

    def unit(r, h):
        n = count_ref[r]
        rows = pl.ds(pl.multiple_of(r * 128, 128), 128)
        cols = [pl.ds(pl.multiple_of(h * 384 + i * 128, 128), 128) for i in range(3)]
        kcol = pl.ds(pl.multiple_of(h * 128, 128), 128)
        vcol = pl.ds(pl.multiple_of(512 + h * 128, 128), 128)
        q = jnp.concatenate([q_ref[rows, c] for c in cols], axis=0)
        do = jnp.concatenate([do_ref[rows, c] for c in cols], axis=0)
        places = [pl.ds(pl.multiple_of(list_ref[r, b] * 128, 128), 128) for b in range(WIDEST)]
        k = jnp.concatenate([kv_ref[w, kcol] for w in places], axis=0)
        v = jnp.concatenate([kv_ref[w, vcol] for w in places], axis=0)
        s = dot_nt(k, q) * FACTOR
        s = jnp.concatenate([s[:256]] + [jnp.where(b < n, s[b * 128:(b + 1) * 128], -1e30)
                                         for b in range(2, WIDEST)], axis=0)
        dprob = dot_nt(v, do)
        e = jnp.exp2(s - jnp.max(s, axis=0, keepdims=True))
        half = e.astype(jnp.bfloat16)
        inverse = 1.0 / jnp.sum(e, axis=0, keepdims=True)
        out_t = dot_tn(v, half) * inverse
        out = out_t.T.astype(jnp.bfloat16)
        for i in range(3):
            att_ref[rows, cols[i]] = out[i * 128:(i + 1) * 128]
        delta = jnp.sum(out_t.astype(jnp.bfloat16).astype(jnp.float32) * do.astype(jnp.float32).T, axis=0,
                        keepdims=True)
        share = jnp.broadcast_to(inverse, (128, 384)).T
        do_share = (do.astype(jnp.float32) * share).astype(jnp.bfloat16)
        q_share = (q.astype(jnp.float32) * (share * SCALE)).astype(jnp.bfloat16)
        ds = (e * (dprob - delta)).astype(jnp.bfloat16)
        dv = dot_nn(half, do_share)
        dk = dot_nn(ds, q_share)
        dq = (dot_tn(k, ds) * (inverse * SCALE)).T.astype(jnp.bfloat16)
        for i in range(3):
            dq_ref[rows, cols[i]] = dq[i * 128:(i + 1) * 128]
        for b, w in enumerate(places):
            piece = slice(b * 128, (b + 1) * 128)
            dkv_ref[w, kcol] = (dkv_ref[w, kcol].astype(jnp.float32) + dk[piece]).astype(jnp.bfloat16)
            dkv_ref[w, vcol] = (dkv_ref[w, vcol].astype(jnp.float32) + dv[piece]).astype(jnp.bfloat16)

    @pl.loop(0, 2)
    def _(r):
        @pl.when(count_ref[r] <= WIDEST)
        def _():
            @pl.loop(0, 4)
            def _(h):
                unit(r, h)

        @pl.when(count_ref[r] > WIDEST)
        def _():
            rows = pl.ds(pl.multiple_of(r * 128, 128), 128)
            att_ref[rows, :] = jnp.zeros((128, 1536), jnp.bfloat16)
            dq_ref[rows, :] = jnp.zeros((128, 1536), jnp.bfloat16)


def attention(block_mask, q, do, wide, kv):
    vm = pl.BlockSpec(memory_space=pltpu.VMEM)
    half = jnp.bfloat16
    return pl.pallas_call(
        attention_kernel,
        out_shape=(jax.ShapeDtypeStruct((256, 1536), half), jax.ShapeDtypeStruct((256, 1536), half),
                   jax.ShapeDtypeStruct((4096, 1024), half), jax.ShapeDtypeStruct((32, 768), half)),
        in_specs=[pl.BlockSpec(memory_space=pltpu.SMEM), vm, vm, vm, vm],
        out_specs=(vm, vm, vm, vm),
        scratch_shapes=[pltpu.VMEM((4096, 128), jnp.float32), pltpu.SMEM((2, 33), jnp.int32),
                        pltpu.SMEM((2,), jnp.int32)],
        compiler_params=pltpu.CompilerParams(vmem_limit_bytes=60 << 20),
        name="attention",
    )(block_mask, q, do, wide, kv)


def grads_kernel(tok_ref, gain_ref, mask_ref, part_dq, part_att, wide_ref, terms, w_all, out_ref, att_ref, w_vm, mine,
                 part, ahead, behind, after, before, relay, crossed, total, dq_ref, wide_box, send_sem, recv_sem,
                 local_sem):
    p = Place()
    net = Net(send_sem, recv_sem)
    greet(p)
    order = [(dz, dy) for dz in (2, 0) for dy in (2, 1, 3, 0)]
    swap, up, down, north, south = p.ids(swap=True), p.ids(dz=1), p.ids(dz=-1), p.ids(dy=1), p.ids(dy=-1)
    loads = {}

    def piece(dy, dz):
        who, _ = p.ids(dy=dy, dz=dz)
        return wide_box.at[who]

    def forward(dz, hops):
        for dy in hops:
            src = wide_ref if dz == 0 else piece(0, 2)
            net.send("w%d%d" % (dz, dy), src, piece(0, dz), p.ids(dy=dy))

    def share():
        net.send("wz", wide_ref, piece(0, 0), p.ids(dz=2))
        forward(0, (1, 3, 2))
        net.send("s00", wide_ref, piece(0, 0), swap)

    def share_far():
        net.recv("wz")
        forward(2, (1, 3, 2))
        net.send("s20", piece(0, 2), piece(0, 2), swap)

    def hand_on():
        for dz in (0, 2):
            for dy in (1, 3, 2):
                net.recv("w%d%d" % (dz, dy))
                net.send("s%d%d" % (dz, dy), piece(-dy, dz), piece(-dy, dz), swap)

    for slot, (dz, dy) in enumerate(order):
        who, _ = p.ids(dy=dy, dz=dz)
        other, _ = p.ids(dy=dy, dz=dz, swap=True)
        net.send("c%d" % slot, terms.at[rows_at(other * 256, 256)], part.at[slot], swap)
        loads[slot] = pltpu.make_async_copy(terms.at[rows_at(who * 256, 256)], mine.at[slot], local_sem.at[slot])
        loads[slot].start()
    weight = pltpu.make_async_copy(w_all, w_vm, local_sem.at[8])
    weight.start()

    def add(dst, *srcs):
        @pl.loop(0, dst.shape[0] // 64)
        def _(t):
            rows = pl.ds(pl.multiple_of(t * 64, 64), 64)
            value = dst[rows, :]
            for src in srcs:
                value = value + src[rows, :]
            dst[rows, :] = value

    def pair(slot):
        loads[slot].wait()
        net.recv("c%d" % slot)
        add(mine.at[slot], part.at[slot])

    def far(base, plane):
        pair(base)
        net.send("a%d" % plane, mine.at[base, :128], ahead.at[plane], north)
        net.send("b%d" % plane, mine.at[base, 128:], behind.at[plane], south)
        pair(base + 1)
        pair(base + 2)

    def near(base, plane):
        net.recv("a%d" % plane)
        add(mine.at[base + 1, :128], ahead.at[plane])
        net.send("f%d" % plane, mine.at[base + 1], after.at[plane], north)
        net.recv("b%d" % plane)
        add(mine.at[base + 2, 128:], behind.at[plane])
        net.send("g%d" % plane, mine.at[base + 2], before.at[plane], south)
        pair(base + 3)

    def gathered(base, plane):
        net.recv("f%d" % plane)
        net.recv("g%d" % plane)
        add(mine.at[base + 3], after.at[plane], before.at[plane])

    def join():
        wide_box[p.i] = wide_ref[...]
        for dz in (0, 2):
            for dy in range(4):
                net.recv("s%d%d" % (dz, dy))
        flags = [chosen(mask_ref, p, r) for r in range(2)]
        for j in range(16):
            cols = slice((j // 4) * 384, (j // 4 + 1) * 384)
            for r in range(2):
                rows = slice(r * 128 + (j % 4) * 32, r * 128 + (j % 4 + 1) * 32)
                for out, local, lo in ((att_ref, part_att, 0), (dq_ref, part_dq, 384)):
                    value = wide_box[j, :, lo:lo + 384].astype(jnp.float32) * flags[r]
                    out[rows, cols] = (local[rows, cols].astype(jnp.float32) + value).astype(jnp.bfloat16)

    def query_part(first, last):
        @pl.loop(first, last)
        def _(t):
            cols = pl.ds(pl.multiple_of(t * 256, 256), 256)
            total[:, cols] = lax.dot_general(dq_ref[...], w_vm[cols, :1536], (((1,), (1,)), ((), ())),
                                             preferred_element_type=jnp.float32)

    far(0, 0)
    far(4, 1)
    share()
    near(0, 0)
    share_far()
    near(4, 1)
    weight.wait()
    gathered(0, 0)
    net.send("h+", mine.at[3, :128], relay.at[0], up)
    net.send("h-", mine.at[3, 128:], relay.at[1], down)
    hand_on()
    net.recv("h+")
    net.send("r+", relay.at[0], crossed.at[:128], up)
    net.recv("h-")
    net.send("r-", relay.at[1], crossed.at[128:], down)
    join()
    query_part(0, 12)
    gathered(4, 1)
    net.recv("r+")
    net.recv("r-")
    add(mine.at[7], crossed)

    @pl.loop(0, 12)
    def _(t):
        cols = pl.ds(pl.multiple_of(t * 256, 256), 256)
        total[:, cols] += lax.dot_general(mine[7], w_vm[cols, 1536:], (((1,), (1,)), ((), ())),
                                          preferred_element_type=jnp.float32)

    @pl.loop(0, 8)
    def _(t):
        rows = pl.ds(pl.multiple_of(t * 32, 32), 32)
        x = tok_ref[rows, :].astype(jnp.float32)
        inv_rms = lax.rsqrt(jnp.mean(x * x, axis=1, keepdims=True) + epsilon)
        scaled = total[rows, :] * gain_ref[...]
        shift = inv_rms * inv_rms * inv_rms * jnp.mean(scaled * x, axis=1, keepdims=True)
        out_ref[rows, :] = (inv_rms * scaled - x * shift).astype(jnp.bfloat16)
    net.drain()


def input_grads(tokens, gain, mask, dq, att, wide, terms, weight):
    vm, anywhere = pl.BlockSpec(memory_space=pltpu.VMEM), pl.BlockSpec(memory_space=pl.ANY)
    half = jnp.bfloat16
    return pl.pallas_call(
        grads_kernel,
        out_shape=(jax.ShapeDtypeStruct((256, 3072), half), jax.ShapeDtypeStruct((256, 1536), half)),
        in_specs=[vm, vm, vm, vm, vm, vm, anywhere, anywhere],
        out_specs=(vm, vm),
        scratch_shapes=[pltpu.VMEM((3072, 2560), half), pltpu.VMEM((8, 256, 1024), half),
                        pltpu.VMEM((8, 256, 1024), half), pltpu.VMEM((2, 128, 1024), half),
                        pltpu.VMEM((2, 128, 1024), half), pltpu.VMEM((2, 256, 1024), half),
                        pltpu.VMEM((2, 256, 1024), half), pltpu.VMEM((2, 128, 1024), half),
                        pltpu.VMEM((256, 1024), half), pltpu.VMEM((256, 3072), jnp.float32),
                        pltpu.VMEM((256, 1536), half), pltpu.VMEM((16, 32, 768), half),
                        pltpu.SemaphoreType.DMA((40,)), pltpu.SemaphoreType.DMA((40,)),
                        pltpu.SemaphoreType.DMA((9,))],
        compiler_params=pltpu.CompilerParams(vmem_limit_bytes=60 << 20, collective_id=1, has_side_effects=True),
        name="input_grads",
    )(tokens, gain, mask, dq, att, wide, terms, weight)


def body(tokens, norm_gain, qkv_weight, block_mask, out_grad):
    gain = norm_gain[None]
    queries, pairs_all, panels, wide = project(tokens[0], gain, block_mask, out_grad[0], qkv_weight)
    part_att, part_dq, block_terms, wide_out = attention(block_mask, queries, out_grad[0], wide, pairs_all)
    token_grad, attended = input_grads(tokens[0], gain, block_mask, part_dq, part_att, wide_out, block_terms, panels)
    return (attended[None], token_grad[None])


def solution(mesh):
    in_specs = (P("fsdp", "ctx", None), P(), P("fsdp", None), P(), P("fsdp", "ctx", None))
    out_specs = (P("fsdp", "ctx", None), P("fsdp", "ctx", None))
    return jax.shard_map(body, mesh=mesh, in_specs=in_specs, out_specs=out_specs, check_vma=False)
```
